32 devices in a mesh: phys: 8 (over y, x, core), ang: 4 (over z).
Axes of the slice: x: 2, y: 2, z: 4, core: 2. Of those that a mesh axis runs over, the one named last changes fastest.
Arguments:
- vorticity: float32 [96, 4, 256, 256], P('ang', None, 'phys'), may hold values from -200 to 200
- forcing_mode: int32 [1], replicated, may hold values from 4 to 85
- time_step: float32 [1], replicated, may hold values from 0.003 to 0.005
- rotation: float32 [1], replicated, may hold values from 0.5 to 3
Outputs:
- residual_modes: float32 [2, 88, 256, 384], P(None, 'phys', 'ang')
The draws below stay inside these ranges and needn't reach their ends.
All inputs are finite; a program needn't handle non-finite values.
Results may differ from the reference program's by a relative error of at most 0.000075.
Values sent between devices are 32-bit elements; how exact they have to be, the bound alone decides.
No kernel may reach another device: no remote copies, remote signals or barrier semaphores. Data moves between devices by JAX's collectives and lax.ppermute only.
A program may use at most 192 MiB of HBM per device.

```python
import math
import jax
import jax.numpy as jnp
from jax import lax

N = 256
A1 = 96
S2 = 4
HALF = 88


def draw_vorticity(key, part):
    count_shape = (A1, S2, 6)
    wave_col = jax.random.randint(jax.random.fold_in(key, 11), count_shape, -6, 7)
    wave_row = jax.random.randint(jax.random.fold_in(key, 12), count_shape, 1, 7)
    phases = jax.random.uniform(jax.random.fold_in(key, 13), count_shape, jnp.float32, -math.pi, math.pi)
    speeds = jax.random.uniform(jax.random.fold_in(key, 16), count_shape, jnp.float32, 0.25, 0.7)
    noise_part = 40.0 * jax.random.truncated_normal(jax.random.fold_in(key, 14), -4.0, 4.0, (A1, S2, N, N), jnp.float32)
    positions = jnp.arange(N, dtype=jnp.int32)
    result_field = noise_part
    for number in range(6):
        col_wave = wave_col[:, :, number][:, :, None, None]
        row_wave = wave_row[:, :, number][:, :, None, None]
        product_mod = jnp.mod(col_wave * positions[None, None, None, :] + row_wave * positions[None, None, :, None], N)
        lengths = jnp.sqrt((col_wave * col_wave + row_wave * row_wave).astype(jnp.float32))
        angle_now = 2.0 * math.pi / N * product_mod.astype(jnp.float32) + phases[:, :, number][:, :, None, None]
        result_field = result_field + speeds[:, :, number][:, :, None, None] * lengths * jnp.cos(angle_now)
    return result_field.astype(jnp.float32)


def setup_inputs(seed: int = 0) -> dict:
    splits = jax.random.split(jax.random.key(seed), 5)
    return {
        "vorticity": draw_vorticity(jax.random.fold_in(splits[4], 71), 0),
        "forcing_mode": jax.random.randint(splits[1], (1,), 4, N // 3 + 1).astype(jnp.int32),
        "time_step": jnp.clip(jax.random.uniform(splits[2], (1,), jnp.float32, 0.003, 0.005), 0.003, 0.005),
        "rotation": jnp.clip(jax.random.uniform(splits[3], (1,), jnp.float32, 0.5, 3.0), 0.5, 3.0),
    }


VISCOSITY = 1.0 / 40.0


def signed_modes(length):
    index = jnp.arange(length)
    return jnp.where(index < length // 2, index, index - length)


def reference(vorticity, forcing_mode, time_step, rotation):
    modes = signed_modes(N).astype(jnp.float32)
    wave_y = modes[:, None]
    wave_x = modes[None, :]
    mode_limit = N // 3
    keep_mask = ((jnp.abs(wave_y) <= mode_limit) & (jnp.abs(wave_x) <= mode_limit)).astype(jnp.float32)
    wave_sq = wave_x * wave_x + wave_y * wave_y
    inverse_sq = jnp.where(wave_sq > 0, 1.0 / jnp.where(wave_sq > 0, wave_sq, 1.0), 0.0)
    forcing = forcing_mode[0].astype(jnp.float32)
    rows_y = 2 * jnp.pi * jnp.arange(N).astype(jnp.float32) / N
    force_rows = (-forcing * jnp.cos(forcing * rows_y))[:, None]
    time_value = time_step[0]
    kept_index = jnp.arange(HALF, dtype=jnp.int32)

    def forward(field):
        return jnp.fft.fft2(field, norm="forward") * keep_mask

    def backward(spectrum):
        return jnp.real(jnp.fft.ifft2(spectrum, norm="forward"))

    def tendency(spectrum):
        stream = spectrum * inverse_sq
        vel_x = backward(1j * wave_y * stream)
        vel_y = backward(-1j * wave_x * stream)
        grad_x = backward(1j * wave_x * spectrum)
        grad_y = backward(1j * wave_y * spectrum)
        return forward(force_rows - (vel_x * grad_x + vel_y * grad_y)) - VISCOSITY * wave_sq * spectrum

    def select(values_in):
        return jnp.take(jnp.swapaxes(values_in, -1, -2), kept_index, axis=-2)

    def one_angle(field):
        spectrum = forward(field)
        section_one = tendency(spectrum)
        second = tendency(spectrum + 0.5 * time_value * section_one)
        advanced = spectrum + time_value * second
        return select(advanced), select(spectrum)

    advanced, start = lax.map(one_angle, vorticity)
    signed_angle = signed_modes(A1).astype(jnp.float32)
    turn = jnp.exp(1j * (signed_angle * rotation[0]))[:, None, None, None]
    result = jnp.fft.fft(advanced, axis=0, norm="ortho") - turn * jnp.fft.fft(start, axis=0, norm="ortho")
    result = jnp.transpose(result, (2, 3, 1, 0)).reshape(HALF, N, S2 * A1)
    return jnp.stack([jnp.real(result), jnp.imag(result)]).astype(jnp.float32)
```

```python
import functools
import math

import jax
import jax.numpy as jnp
import ml_dtypes
import numpy as np
from jax import lax
from jax.experimental import pallas as pl
from jax.experimental.pallas import tpu as pltpu
from jax.sharding import PartitionSpec as P

VISCOSITY = 1.0 / 40.0
F32 = jnp.float32
BF16 = jnp.bfloat16


def split_table(table):
    table = np.asarray(table, np.float32)
    high = table.astype(ml_dtypes.bfloat16)
    low = (table - high.astype(np.float32)).astype(ml_dtypes.bfloat16)
    return high, low


def signed(values, length):
    return np.where(values < length // 2, values, values - length)


def make_tables(width, phys, ang):
    limit = width // 3
    half = width // 2
    plus = (limit + phys) // phys
    slots = plus
    while (slots * phys) % 16 or (phys == 8 and slots * 12 % 8):
        slots += 1
    slot = np.arange(slots * phys)
    kx = np.where(slot % slots < plus, (slot // slots) * plus + slot % slots, -1)
    kx_keep = ((kx >= 0) & (kx <= limit)).astype(np.float64)
    kx = np.maximum(kx, 0)
    block = width // ang
    lane = np.arange(width)
    owner = lane // block
    part = (lane % block) // (block // 2)
    even_index = owner * block + 2 * (lane % (block // 2))
    turn = 2.0 * math.pi / width
    grid = np.arange(width)

    def angle(left, right):
        return turn * np.mod(left[:, None] * right[None, :], width)

    x_turn = angle(kx, grid)
    fwd_x = np.concatenate([np.cos(x_turn), -np.sin(x_turn)]) / width
    fwd_x = fwd_x * np.concatenate([kx_keep, kx_keep])[:, None]
    weight = (np.where(kx == 0, 1.0, 2.0) * kx_keep)[:, None]
    inv_x = np.concatenate([weight * np.cos(x_turn), -weight * np.sin(x_turn)]).T
    inv_kx = np.concatenate(
        [-weight * kx[:, None] * np.sin(x_turn), -weight * kx[:, None] * np.cos(x_turn)]
    ).T
    fwd_y, inv_y, lane_ky = [], [], []
    for parity in (0, 1):
        ky = signed(even_index + parity, width)
        keep = (np.abs(ky) <= limit).astype(np.float64)
        lane_ky.append(ky)
        y_turn = angle(np.arange(half), ky)
        cos_y, sin_y = np.cos(y_turn) * keep, np.sin(y_turn) * keep
        real_out = part == 0
        from_real = np.where(real_out, cos_y, -sin_y)
        from_imag = np.where(real_out, sin_y, cos_y)
        fwd_y.append(np.concatenate([from_real, from_imag]) / width)
        real_back = np.where(real_out, cos_y, -sin_y).T
        imag_back = np.where(real_out, sin_y, cos_y).T
        scale = ky[:, None]
        inv_y.append(
            np.concatenate(
                [real_back, imag_back, -scale * imag_back, scale * real_back], axis=1
            )
        )
    lanes = np.concatenate(lane_ky).astype(np.float32)
    wave_sq = kx.astype(np.float32)[:, None] ** 2 + lanes[None, :] ** 2
    inverse_sq = np.where(wave_sq > 0, 1.0 / np.where(wave_sq > 0, wave_sq, 1.0), 0.0)
    return dict(
        plus=plus,
        slots=slots,
        fwd_x=split_table(fwd_x),
        inv_x=split_table(inv_x),
        inv_kx=split_table(inv_kx),
        fwd_y=[split_table(t) for t in fwd_y],
        inv_y=[split_table(t) for t in inv_y],
        inverse_sq=inverse_sq.astype(np.float32),
        damping=(np.float32(VISCOSITY) * wave_sq).astype(np.float32),
    )


def split(values):
    high = values.astype(BF16)
    low = (values - high.astype(F32)).astype(BF16)
    return high, low


def right_mul(values, high_ref, low_ref):
    high, low = split(values)
    left = jnp.concatenate([high, low, high], axis=1)
    right = jnp.concatenate([high_ref[...], high_ref[...], low_ref[...]], axis=0)
    return jnp.dot(left, right, preferred_element_type=F32)


def left_mul(high_ref, low_ref, values):
    high, low = split(values)
    left = jnp.concatenate([high_ref[...], low_ref[...], high_ref[...]], axis=1)
    right = jnp.concatenate([high, high, low], axis=0)
    return jnp.dot(left, right, preferred_element_type=F32)


def forward_y(rows, tables):
    count = rows.shape[0] // 2
    half = rows.shape[1] // 2
    real, imag = rows[:count], rows[count:]
    even = jnp.concatenate(
        [real[:, :half] + real[:, half:], imag[:, :half] + imag[:, half:]], axis=1
    )
    odd = jnp.concatenate(
        [real[:, :half] - real[:, half:], imag[:, :half] - imag[:, half:]], axis=1
    )
    return jnp.concatenate(
        [right_mul(even, tables[0], tables[1]), right_mul(odd, tables[2], tables[3])], axis=1
    )


def store_send(send_ref, modes, field, field_count, interleave):
    count = modes.shape[0]
    pieces = [modes[:, 128 * b : 128 * (b + 1)] for b in range(4)]
    if interleave:
        low_lane = lax.broadcasted_iota(jnp.int32, pieces[0].shape, 1) < 64
        out = []
        for b in range(2):
            even, odd = pieces[b], pieces[b + 2]
            out.append(jnp.where(low_lane, even, pltpu.roll(odd, 64, 1)))
            out.append(jnp.where(low_lane, pltpu.roll(even, 64, 1), odd))
        pieces = out
    for b in range(4):
        send_ref[b, pl.ds(field, count, stride=field_count), :] = pieces[b]


def spectrum_kernel(interleave, field_count, x_ref, fx_hi, fx_lo, e_hi, e_lo, o_hi, o_lo, s_ref, send_ref):
    width = x_ref.shape[3]
    grid_field = x_ref[:, 0].reshape(width, width)
    high, low = split(grid_field)
    left = jnp.concatenate([fx_hi[...], fx_lo[...], fx_hi[...]], axis=1)
    right = jnp.concatenate([high, high, low], axis=1)
    rows = lax.dot_general(left, right, (((1,), (1,)), ((), ())), preferred_element_type=F32)
    modes = forward_y(rows, (e_hi, e_lo, o_hi, o_lo))
    s_ref[0] = modes
    store_send(send_ref, modes, pl.program_id(0), field_count, interleave)


def advance_kernel(
    interleave,
    field_count,
    dt_ref,
    s_ref,
    force_ref,
    isq_ref,
    damp_ref,
    fx_hi,
    fx_lo,
    e_hi,
    e_lo,
    o_hi,
    o_lo,
    bx_hi,
    bx_lo,
    bk_hi,
    bk_lo,
    ye_hi,
    ye_lo,
    yo_hi,
    yo_lo,
    send_ref,
):
    spectrum = s_ref[0]
    count = spectrum.shape[0]
    width = spectrum.shape[1] // 2
    half = width // 2

    def tendency(modes):
        both = jnp.concatenate([modes * isq_ref[...], modes], axis=0)
        even = right_mul(both[:, :width], ye_hi, ye_lo)
        odd = right_mul(both[:, width:], yo_hi, yo_lo)
        first, second = even + odd, even - odd

        def columns(row, block):
            rows = slice(row * count, (row + 1) * count)
            real = slice(2 * block * half, (2 * block + 1) * half)
            imag = slice((2 * block + 1) * half, (2 * block + 2) * half)
            return jnp.concatenate(
                [
                    jnp.concatenate([first[rows, real], second[rows, real]], axis=1),
                    jnp.concatenate([first[rows, imag], second[rows, imag]], axis=1),
                ],
                axis=0,
            )

        vel_x = left_mul(bx_hi, bx_lo, columns(0, 1))
        grad_x = left_mul(bk_hi, bk_lo, columns(1, 0))
        total = vel_x * grad_x
        minus_vel_y = left_mul(bk_hi, bk_lo, columns(0, 0))
        grad_y = left_mul(bx_hi, bx_lo, columns(1, 1))
        total = force_ref[...] - (total - minus_vel_y * grad_y)
        rows = left_mul(fx_hi, fx_lo, total)
        return forward_y(rows, (e_hi, e_lo, o_hi, o_lo)) - damp_ref[...] * modes

    step = dt_ref[0]
    middle = spectrum + (0.5 * step) * tendency(spectrum)
    advanced = spectrum + step * tendency(middle)
    store_send(send_ref, advanced, pl.program_id(0), field_count, interleave)


def angle_kernel(field_count, slots, adv_ref, start_ref, mat_hi, mat_lo, turn_ref, out_ref, rows_ref):
    sources = adv_ref.shape[0] // (slots * field_count)
    base = pl.program_id(0) * field_count

    def gather(ref):
        rows = [
            ref[pl.ds(base + f, sources, stride=slots * field_count), :] for f in range(field_count)
        ]
        return jnp.concatenate(rows, axis=0).T

    both = jnp.concatenate([gather(adv_ref), gather(start_ref)], axis=0)
    result = right_mul(both, mat_hi, mat_lo)
    lanes = adv_ref.shape[1]
    quarter = lanes // 4
    merged = result.shape[1] // 2
    turn_cos, turn_sin = turn_ref[0:1], turn_ref[1:2]

    def modes(row):
        real = result[row : row + quarter]
        imag = result[row + quarter : row + 2 * quarter]
        return (
            real[:, :merged] + imag[:, merged:],
            imag[:, :merged] - real[:, merged:],
        )

    blocks = merged // 128
    for parity in range(2):
        adv_real, adv_imag = modes(parity * 2 * quarter)
        real, imag = modes(lanes + parity * 2 * quarter)
        pair = (
            adv_real - (turn_cos * real - turn_sin * imag),
            adv_imag - (turn_sin * real + turn_cos * imag),
        )
        for part in range(2):
            for b in range(blocks):
                rows_ref[part * blocks + b, pl.ds(parity, quarter, stride=2), :] = pair[part][
                    :, 128 * b : 128 * (b + 1)
                ]
    for part in range(2):
        out_ref[part, 0] = jnp.concatenate(
            [rows_ref[part * blocks + b] for b in range(blocks)], axis=1
        )


def whole_spec(shape):
    zeros = (0,) * len(shape)
    return pl.BlockSpec(tuple(shape), lambda *_: zeros)


def local(tables, vorticity, forcing_mode, time_step, rotation):
    angle_local, samples, row_count, width = vorticity.shape
    phys = lax.axis_size("phys")
    ang = lax.axis_size("ang")
    angle_total = angle_local * ang
    group_fields = angle_local * samples
    field_count = -(-group_fields // phys)
    slots, plus = tables["slots"], tables["plus"]
    count = slots * phys
    block = width // ang
    interleave = block == 64

    forcing = forcing_mode[0].astype(F32)
    rows_global = jnp.arange(width, dtype=jnp.int32).astype(F32)
    force = (-forcing * jnp.cos(forcing * (2 * jnp.pi * rows_global / width)))[None, :]

    fields = vorticity.reshape(group_fields, row_count, width)
    if field_count * phys != group_fields:
        fields = jnp.pad(fields, ((0, field_count * phys - group_fields), (0, 0), (0, 0)))
    fields = fields.reshape(phys, field_count, row_count, width)
    fields = lax.all_to_all(fields, "phys", split_axis=0, concat_axis=0, tiled=True)

    fwd = list(tables["fwd_x"]) + list(tables["fwd_y"][0]) + list(tables["fwd_y"][1])
    fwd = [jnp.asarray(t) for t in fwd]
    inv = list(tables["inv_x"]) + list(tables["inv_kx"]) + list(tables["inv_y"][0]) + list(tables["inv_y"][1])
    inv = [jnp.asarray(t) for t in inv]
    params = pltpu.CompilerParams(
        dimension_semantics=("arbitrary",), vmem_limit_bytes=56 * 1024 * 1024
    )
    send_shape = (4, count * field_count, 128)
    start_modes, start_send = pl.pallas_call(
        functools.partial(spectrum_kernel, interleave, field_count),
        grid=(field_count,),
        in_specs=[pl.BlockSpec((phys, 1, row_count, width), lambda f: (0, f, 0, 0))]
        + [whole_spec(t.shape) for t in fwd],
        out_specs=[
            pl.BlockSpec((1, count, 2 * width), lambda f: (f, 0, 0)),
            whole_spec(send_shape),
        ],
        out_shape=[
            jax.ShapeDtypeStruct((field_count, count, 2 * width), F32),
            jax.ShapeDtypeStruct(send_shape, F32),
        ],
        compiler_params=params,
        name="spectrum",
    )(fields, *fwd)

    def exchange(send):
        rows = slots * field_count
        if interleave:
            send = send.reshape(ang * phys, rows, 128)
        else:
            send = send.reshape(2, 2, phys, rows, 128 // block, block)
            send = send.transpose(1, 4, 2, 3, 0, 5).reshape(ang * phys, rows, 2 * block)
        got = lax.all_to_all(send, ("ang", "phys"), split_axis=0, concat_axis=0, tiled=True)
        return got.reshape(ang * phys * rows, 2 * block)

    start = exchange(start_send)

    extra = [force, jnp.asarray(tables["inverse_sq"]), jnp.asarray(tables["damping"])]
    adv_send = pl.pallas_call(
        functools.partial(advance_kernel, interleave, field_count),
        grid=(field_count,),
        in_specs=[
            pl.BlockSpec(memory_space=pltpu.SMEM),
            pl.BlockSpec((1, count, 2 * width), lambda f: (f, 0, 0)),
        ]
        + [whole_spec(t.shape) for t in extra + fwd + inv],
        out_specs=whole_spec(send_shape),
        out_shape=jax.ShapeDtypeStruct(send_shape, F32),
        compiler_params=params,
        name="advance",
    )(time_step, start_modes, *extra, *fwd, *inv)
    advanced = exchange(adv_send)

    index = np.arange(field_count)[:, None] + field_count * np.arange(phys)[None, :]
    index = np.broadcast_to(index[:, None, :], (field_count, ang, phys))
    first = np.arange(ang)[None, :, None] * angle_local + index // samples
    valid = index < group_fields
    turn = 2.0 * math.pi / angle_total * np.mod(
        first[..., None] * np.arange(angle_total), angle_total
    )
    scale = 1.0 / math.sqrt(angle_total)
    pair = scale * np.stack([np.cos(turn), np.sin(turn)], axis=-2)
    pick = ((index % samples)[..., None] == np.arange(samples)) & valid[..., None]
    pick = jnp.asarray(pick.reshape(-1, 1, samples, 1).astype(ml_dtypes.bfloat16))
    mat_hi, mat_lo = [
        (jnp.asarray(part.reshape(-1, 2, 1, angle_total)) * pick).reshape(
            -1, 2 * samples * angle_total
        )
        for part in split_table(pair)
    ]
    signed_angle = jnp.asarray(signed(np.arange(angle_total), angle_total).astype(np.float32))
    turns = jnp.stack(
        [
            jnp.tile(jnp.cos(signed_angle * rotation[0]), samples),
            jnp.tile(jnp.sin(signed_angle * rotation[0]), samples),
        ]
    )
    merged = samples * angle_total
    return pl.pallas_call(
        functools.partial(angle_kernel, field_count, slots),
        grid=(plus,),
        in_specs=[
            whole_spec(t.shape) for t in (advanced, start, mat_hi, mat_lo, turns)
        ],
        out_specs=pl.BlockSpec((2, 1, block, merged), lambda k: (0, k, 0, 0)),
        out_shape=jax.ShapeDtypeStruct((2, plus, block, merged), F32),
        scratch_shapes=[pltpu.VMEM((2 * merged // 128, block, 128), F32)],
        compiler_params=params,
        name="angle",
    )(advanced, start, mat_hi, mat_lo, turns)


def solution(mesh):
    in_specs = (P("ang", None, "phys", None), P(), P(), P())
    out_specs = P(None, "phys", "ang", None)

    def program(vorticity, forcing_mode, time_step, rotation):
        tables = make_tables(vorticity.shape[3], mesh.shape["phys"], mesh.shape["ang"])
        return jax.shard_map(
            functools.partial(local, tables),
            mesh=mesh,
            in_specs=in_specs,
            out_specs=out_specs,
            check_vma=False,
        )(vorticity, forcing_mode, time_step, rotation)

    return program
```

```python
import functools
import math

import jax
import jax.numpy as jnp
import ml_dtypes
import numpy as np
from jax import lax
from jax.experimental import pallas as pl
from jax.experimental.pallas import tpu as pltpu
from jax.sharding import PartitionSpec as P

VISCOSITY = 1.0 / 40.0
F32 = jnp.float32
BF16 = jnp.bfloat16


def split_table(table):
    table = np.asarray(table, np.float32)
    high = table.astype(ml_dtypes.bfloat16)
    low = (table - high.astype(np.float32)).astype(ml_dtypes.bfloat16)
    return high, low


def signed(values, length):
    return np.where(values < length // 2, values, values - length)


def make_tables(width, phys, ang):
    limit = width // 3
    half = width // 2
    plus = (limit + phys) // phys
    slots = plus
    while (slots * phys) % 16 or (phys == 8 and slots * 12 % 8):
        slots += 1
    slot = np.arange(slots * phys)
    kx = np.where(slot % slots < plus, (slot // slots) * plus + slot % slots, -1)
    kx_keep = ((kx >= 0) & (kx <= limit)).astype(np.float64)
    kx = np.maximum(kx, 0)
    block = width // ang
    lane = np.arange(width)
    owner = lane // block
    part = (lane % block) // (block // 2)
    even_index = owner * block + 2 * (lane % (block // 2))
    turn = 2.0 * math.pi / width
    grid = np.arange(width)

    def angle(left, right):
        return turn * np.mod(left[:, None] * right[None, :], width)

    x_turn = angle(kx, grid)
    fwd_x = np.concatenate([np.cos(x_turn), -np.sin(x_turn)]) / width
    fwd_x = fwd_x * np.concatenate([kx_keep, kx_keep])[:, None]
    weight = (np.where(kx == 0, 1.0, 2.0) * kx_keep)[:, None]
    inv_x = np.concatenate([weight * np.cos(x_turn), -weight * np.sin(x_turn)]).T
    inv_kx = np.concatenate(
        [-weight * kx[:, None] * np.sin(x_turn), -weight * kx[:, None] * np.cos(x_turn)]
    ).T
    fwd_y, inv_y, lane_ky = [], [], []
    for parity in (0, 1):
        ky = signed(even_index + parity, width)
        keep = (np.abs(ky) <= limit).astype(np.float64)
        lane_ky.append(ky)
        y_turn = angle(np.arange(half), ky)
        cos_y, sin_y = np.cos(y_turn) * keep, np.sin(y_turn) * keep
        real_out = part == 0
        from_real = np.where(real_out, cos_y, -sin_y)
        from_imag = np.where(real_out, sin_y, cos_y)
        fwd_y.append(np.concatenate([from_real, from_imag]) / width)
        real_back = np.where(real_out, cos_y, -sin_y).T
        imag_back = np.where(real_out, sin_y, cos_y).T
        scale = ky[:, None]
        inv_y.append(
            np.concatenate(
                [real_back, imag_back, -scale * imag_back, scale * real_back], axis=1
            )
        )
    lanes = np.concatenate(lane_ky).astype(np.float32)
    wave_sq = kx.astype(np.float32)[:, None] ** 2 + lanes[None, :] ** 2
    inverse_sq = np.where(wave_sq > 0, 1.0 / np.where(wave_sq > 0, wave_sq, 1.0), 0.0)
    return dict(
        plus=plus,
        slots=slots,
        fwd_x=split_table(fwd_x),
        inv_x=split_table(inv_x),
        inv_kx=split_table(inv_kx),
        fwd_y=[split_table(t) for t in fwd_y],
        inv_y=[split_table(t) for t in inv_y],
        inverse_sq=inverse_sq.astype(np.float32),
        damping=(np.float32(VISCOSITY) * wave_sq).astype(np.float32),
    )


def split(values):
    high = values.astype(BF16)
    low = (values - high.astype(F32)).astype(BF16)
    return high, low


def right_mul(values, high_ref, low_ref):
    high, low = split(values)
    left = jnp.concatenate([high, low, high], axis=1)
    right = jnp.concatenate([high_ref[...], high_ref[...], low_ref[...]], axis=0)
    return jnp.dot(left, right, preferred_element_type=F32)


def left_mul(high_ref, low_ref, values):
    high, low = split(values)
    left = jnp.concatenate([high_ref[...], low_ref[...], high_ref[...]], axis=1)
    right = jnp.concatenate([high, high, low], axis=0)
    return jnp.dot(left, right, preferred_element_type=F32)


def forward_y(rows, tables):
    count = rows.shape[0] // 2
    half = rows.shape[1] // 2
    real, imag = rows[:count], rows[count:]
    even = jnp.concatenate(
        [real[:, :half] + real[:, half:], imag[:, :half] + imag[:, half:]], axis=1
    )
    odd = jnp.concatenate(
        [real[:, :half] - real[:, half:], imag[:, :half] - imag[:, half:]], axis=1
    )
    return jnp.concatenate(
        [right_mul(even, tables[0], tables[1]), right_mul(odd, tables[2], tables[3])], axis=1
    )


def store_send(send_ref, modes, field, field_count, interleave):
    count = modes.shape[0]
    pieces = [modes[:, 128 * b : 128 * (b + 1)] for b in range(4)]
    if interleave:
        low_lane = lax.broadcasted_iota(jnp.int32, pieces[0].shape, 1) < 64
        out = []
        for b in range(2):
            even, odd = pieces[b], pieces[b + 2]
            out.append(jnp.where(low_lane, even, pltpu.roll(odd, 64, 1)))
            out.append(jnp.where(low_lane, pltpu.roll(even, 64, 1), odd))
        pieces = out
    for b in range(4):
        send_ref[b, pl.ds(field, count, stride=field_count), :] = pieces[b]


def spectrum_kernel(interleave, field_count, x_ref, fx_hi, fx_lo, e_hi, e_lo, o_hi, o_lo, s_ref, send_ref):
    width = x_ref.shape[3]
    grid_field = x_ref[:, 0].reshape(width, width)
    high, low = split(grid_field)
    left = jnp.concatenate([fx_hi[...], fx_lo[...], fx_hi[...]], axis=1)
    right = jnp.concatenate([high, high, low], axis=1)
    rows = lax.dot_general(left, right, (((1,), (1,)), ((), ())), preferred_element_type=F32)
    modes = forward_y(rows, (e_hi, e_lo, o_hi, o_lo))
    s_ref[0] = modes
    store_send(send_ref, modes, pl.program_id(0), field_count, interleave)


def advance_kernel(
    interleave,
    field_count,
    dt_ref,
    s_ref,
    force_ref,
    isq_ref,
    damp_ref,
    fx_hi,
    fx_lo,
    e_hi,
    e_lo,
    o_hi,
    o_lo,
    bx_hi,
    bx_lo,
    bk_hi,
    bk_lo,
    ye_hi,
    ye_lo,
    yo_hi,
    yo_lo,
    send_ref,
):
    spectrum = s_ref[0]
    count = spectrum.shape[0]
    width = spectrum.shape[1] // 2
    half = width // 2

    def tendency(modes):
        both = jnp.concatenate([modes * isq_ref[...], modes], axis=0)
        even = right_mul(both[:, :width], ye_hi, ye_lo)
        odd = right_mul(both[:, width:], yo_hi, yo_lo)
        first, second = even + odd, even - odd

        def columns(row, block):
            rows = slice(row * count, (row + 1) * count)
            real = slice(2 * block * half, (2 * block + 1) * half)
            imag = slice((2 * block + 1) * half, (2 * block + 2) * half)
            return jnp.concatenate(
                [
                    jnp.concatenate([first[rows, real], second[rows, real]], axis=1),
                    jnp.concatenate([first[rows, imag], second[rows, imag]], axis=1),
                ],
                axis=0,
            )

        vel_x = left_mul(bx_hi, bx_lo, columns(0, 1))
        grad_x = left_mul(bk_hi, bk_lo, columns(1, 0))
        total = vel_x * grad_x
        minus_vel_y = left_mul(bk_hi, bk_lo, columns(0, 0))
        grad_y = left_mul(bx_hi, bx_lo, columns(1, 1))
        total = force_ref[...] - (total - minus_vel_y * grad_y)
        rows = left_mul(fx_hi, fx_lo, total)
        return forward_y(rows, (e_hi, e_lo, o_hi, o_lo)) - damp_ref[...] * modes

    step = dt_ref[0]
    middle = spectrum + (0.5 * step) * tendency(spectrum)
    advanced = spectrum + step * tendency(middle)
    store_send(send_ref, advanced, pl.program_id(0), field_count, interleave)


def angle_kernel(field_count, slots, adv_ref, start_ref, mat_hi, mat_lo, turn_ref, out_ref, rows_ref):
    sources = adv_ref.shape[0] // (slots * field_count)
    base = pl.program_id(0) * field_count

    def gather(ref):
        rows = [
            ref[pl.ds(base + f, sources, stride=slots * field_count), :] for f in range(field_count)
        ]
        return jnp.concatenate(rows, axis=0).T

    both = jnp.concatenate([gather(adv_ref), gather(start_ref)], axis=0)
    result = right_mul(both, mat_hi, mat_lo)
    lanes = adv_ref.shape[1]
    quarter = lanes // 4
    merged = result.shape[1] // 2
    turn_cos, turn_sin = turn_ref[0:1], turn_ref[1:2]

    def modes(row):
        real = result[row : row + quarter]
        imag = result[row + quarter : row + 2 * quarter]
        return (
            real[:, :merged] + imag[:, merged:],
            imag[:, :merged] - real[:, merged:],
        )

    blocks = merged // 128
    for parity in range(2):
        adv_real, adv_imag = modes(parity * 2 * quarter)
        real, imag = modes(lanes + parity * 2 * quarter)
        pair = (
            adv_real - (turn_cos * real - turn_sin * imag),
            adv_imag - (turn_sin * real + turn_cos * imag),
        )
        for part in range(2):
            for b in range(blocks):
                rows_ref[part * blocks + b, pl.ds(parity, quarter, stride=2), :] = pair[part][
                    :, 128 * b : 128 * (b + 1)
                ]
    for part in range(2):
        out_ref[part, 0] = jnp.concatenate(
            [rows_ref[part * blocks + b] for b in range(blocks)], axis=1
        )


def cost(flops):
    return pl.CostEstimate(flops=int(flops), bytes_accessed=8 * 1024 * 1024, transcendentals=0)


def whole_spec(shape):
    zeros = (0,) * len(shape)
    return pl.BlockSpec(tuple(shape), lambda *_: zeros)


def local(tables, vorticity, forcing_mode, time_step, rotation):
    angle_local, samples, row_count, width = vorticity.shape
    phys = lax.axis_size("phys")
    ang = lax.axis_size("ang")
    angle_total = angle_local * ang
    group_fields = angle_local * samples
    field_count = -(-group_fields // phys)
    slots, plus = tables["slots"], tables["plus"]
    count = slots * phys
    block = width // ang
    interleave = block == 64

    forcing = forcing_mode[0].astype(F32)
    rows_global = jnp.arange(width, dtype=jnp.int32).astype(F32)
    force = (-forcing * jnp.cos(forcing * (2 * jnp.pi * rows_global / width)))[None, :]

    fields = vorticity.reshape(group_fields, row_count, width)
    if field_count * phys != group_fields:
        fields = jnp.pad(fields, ((0, field_count * phys - group_fields), (0, 0), (0, 0)))
    fields = fields.reshape(phys, field_count, row_count, width)
    fields = lax.all_to_all(fields, "phys", split_axis=0, concat_axis=0, tiled=True)

    fwd = list(tables["fwd_x"]) + list(tables["fwd_y"][0]) + list(tables["fwd_y"][1])
    fwd = [jnp.asarray(t) for t in fwd]
    inv = list(tables["inv_x"]) + list(tables["inv_kx"]) + list(tables["inv_y"][0]) + list(tables["inv_y"][1])
    inv = [jnp.asarray(t) for t in inv]
    params = pltpu.CompilerParams(
        dimension_semantics=("arbitrary",), vmem_limit_bytes=56 * 1024 * 1024
    )
    send_shape = (4, count * field_count, 128)
    start_modes, start_send = pl.pallas_call(
        functools.partial(spectrum_kernel, interleave, field_count),
        grid=(field_count,),
        in_specs=[pl.BlockSpec((phys, 1, row_count, width), lambda f: (0, f, 0, 0))]
        + [whole_spec(t.shape) for t in fwd],
        out_specs=[
            pl.BlockSpec((1, count, 2 * width), lambda f: (f, 0, 0)),
            whole_spec(send_shape),
        ],
        out_shape=[
            jax.ShapeDtypeStruct((field_count, count, 2 * width), F32),
            jax.ShapeDtypeStruct(send_shape, F32),
        ],
        cost_estimate=cost(field_count * 4 * count * 6 * width * width),
        compiler_params=params,
        name="spectrum",
    )(fields, *fwd)

    def exchange(send):
        rows = slots * field_count
        if interleave:
            send = send.reshape(ang * phys, rows, 128)
        else:
            send = send.reshape(2, 2, phys, rows, 128 // block, block)
            send = send.transpose(1, 4, 2, 3, 0, 5).reshape(ang * phys, rows, 2 * block)
        got = lax.all_to_all(send, ("ang", "phys"), split_axis=0, concat_axis=0, tiled=True)
        return got.reshape(ang * phys * rows, 2 * block)

    start = exchange(start_send)

    extra = [force, jnp.asarray(tables["inverse_sq"]), jnp.asarray(tables["damping"])]
    adv_send = pl.pallas_call(
        functools.partial(advance_kernel, interleave, field_count),
        grid=(field_count,),
        in_specs=[
            pl.BlockSpec(memory_space=pltpu.SMEM),
            pl.BlockSpec((1, count, 2 * width), lambda f: (f, 0, 0)),
        ]
        + [whole_spec(t.shape) for t in extra + fwd + inv],
        out_specs=whole_spec(send_shape),
        out_shape=jax.ShapeDtypeStruct(send_shape, F32),
        cost_estimate=cost(field_count * 24 * count * 6 * width * width),
        compiler_params=params,
        name="advance",
    )(time_step, start_modes, *extra, *fwd, *inv)
    adv_send, start = lax.optimization_barrier((adv_send, start))
    advanced = exchange(adv_send)

    index = np.arange(field_count)[:, None] + field_count * np.arange(phys)[None, :]
    index = np.broadcast_to(index[:, None, :], (field_count, ang, phys))
    first = np.arange(ang)[None, :, None] * angle_local + index // samples
    valid = index < group_fields
    turn = 2.0 * math.pi / angle_total * np.mod(
        first[..., None] * np.arange(angle_total), angle_total
    )
    scale = 1.0 / math.sqrt(angle_total)
    pair = scale * np.stack([np.cos(turn), np.sin(turn)], axis=-2)
    pick = ((index % samples)[..., None] == np.arange(samples)) & valid[..., None]
    pick = jnp.asarray(pick.reshape(-1, 1, samples, 1).astype(ml_dtypes.bfloat16))
    mat_hi, mat_lo = [
        (jnp.asarray(part.reshape(-1, 2, 1, angle_total)) * pick).reshape(
            -1, 2 * samples * angle_total
        )
        for part in split_table(pair)
    ]
    signed_angle = jnp.asarray(signed(np.arange(angle_total), angle_total).astype(np.float32))
    turns = jnp.stack(
        [
            jnp.tile(jnp.cos(signed_angle * rotation[0]), samples),
            jnp.tile(jnp.sin(signed_angle * rotation[0]), samples),
        ]
    )
    merged = samples * angle_total
    return pl.pallas_call(
        functools.partial(angle_kernel, field_count, slots),
        grid=(plus,),
        in_specs=[
            whole_spec(t.shape) for t in (advanced, start, mat_hi, mat_lo, turns)
        ],
        out_specs=pl.BlockSpec((2, 1, block, merged), lambda k: (0, k, 0, 0)),
        out_shape=jax.ShapeDtypeStruct((2, plus, block, merged), F32),
        scratch_shapes=[pltpu.VMEM((2 * merged // 128, block, 128), F32)],
        cost_estimate=cost(plus * 4 * block * 6 * advanced.shape[0] // (slots) * merged // 100),
        compiler_params=params,
        name="angle",
    )(advanced, start, mat_hi, mat_lo, turns)


def solution(mesh):
    in_specs = (P("ang", None, "phys", None), P(), P(), P())
    out_specs = P(None, "phys", "ang", None)

    def program(vorticity, forcing_mode, time_step, rotation):
        tables = make_tables(vorticity.shape[3], mesh.shape["phys"], mesh.shape["ang"])
        return jax.shard_map(
            functools.partial(local, tables),
            mesh=mesh,
            in_specs=in_specs,
            out_specs=out_specs,
            check_vma=False,
        )(vorticity, forcing_mode, time_step, rotation)

    return program
```

```python
import functools
import math

import jax
import jax.numpy as jnp
import ml_dtypes
import numpy as np
from jax import lax
from jax.experimental import pallas as pl
from jax.experimental.pallas import tpu as pltpu
from jax.sharding import PartitionSpec as P

VISCOSITY = 1.0 / 40.0
F32 = jnp.float32
BF16 = jnp.bfloat16


def split_table(table):
    table = np.asarray(table, np.float32)
    high = table.astype(ml_dtypes.bfloat16)
    low = (table - high.astype(np.float32)).astype(ml_dtypes.bfloat16)
    return high, low


def signed(values, length):
    return np.where(values < length // 2, values, values - length)


def make_tables(width, phys, ang):
    limit = width // 3
    half = width // 2
    plus = (limit + phys) // phys
    count = plus * phys
    full = 8 * phys * (plus // 8)
    row = np.arange(count)
    rest = plus % 8
    kx = np.where(
        row < full,
        (row % max(full, 1)) // 8 // max(plus // 8, 1) * plus + row % (8 * max(plus // 8, 1)),
        (row - full) // max(rest, 1) * plus + plus - rest + (row - full) % max(rest, 1),
    )
    kx_keep = (kx <= limit).astype(np.float64)
    block = width // ang
    lane = np.arange(width)
    owner = lane // block
    part = (lane % block) // (block // 2)
    even_index = owner * block + 2 * (lane % (block // 2))
    turn = 2.0 * math.pi / width
    grid = np.arange(width)

    def angle(left, right):
        return turn * np.mod(left[:, None] * right[None, :], width)

    x_turn = angle(kx, grid)
    fwd_x = np.concatenate([np.cos(x_turn), -np.sin(x_turn)]) / width
    fwd_x = fwd_x * np.concatenate([kx_keep, kx_keep])[:, None]
    weight = (np.where(kx == 0, 1.0, 2.0) * kx_keep)[:, None]
    inv_x = np.concatenate([weight * np.cos(x_turn), -weight * np.sin(x_turn)]).T
    inv_kx = np.concatenate(
        [-weight * kx[:, None] * np.sin(x_turn), -weight * kx[:, None] * np.cos(x_turn)]
    ).T
    fwd_y, inv_y, lane_ky = [], [], []
    for parity in (0, 1):
        ky = signed(even_index + parity, width)
        keep = (np.abs(ky) <= limit).astype(np.float64)
        lane_ky.append(ky)
        y_turn = angle(np.arange(half), ky)
        cos_y, sin_y = np.cos(y_turn) * keep, np.sin(y_turn) * keep
        real_out = part == 0
        from_real = np.where(real_out, cos_y, -sin_y)
        from_imag = np.where(real_out, sin_y, cos_y)
        fwd_y.append(np.concatenate([from_real, from_imag]) / width)
        real_back = np.where(real_out, cos_y, -sin_y).T
        imag_back = np.where(real_out, sin_y, cos_y).T
        scale = ky[:, None]
        inv_y.append(
            np.concatenate(
                [real_back, imag_back, -scale * imag_back, scale * real_back], axis=1
            )
        )
    return dict(
        plus=plus,
        fwd_x=split_table(fwd_x),
        inv_x=split_table(inv_x),
        inv_kx=split_table(inv_kx),
        fwd_y=[split_table(t) for t in fwd_y],
        inv_y=[split_table(t) for t in inv_y],
        wave_x=kx.astype(np.float32)[:, None],
        wave_y=np.concatenate(lane_ky).astype(np.float32)[None, :],
    )


def split(values):
    high = values.astype(BF16)
    low = (values - high.astype(F32)).astype(BF16)
    return high, low


def right_mul(values, high_ref, low_ref):
    high, low = split(values)
    left = jnp.concatenate([high, low, high], axis=1)
    right = jnp.concatenate([high_ref[...], high_ref[...], low_ref[...]], axis=0)
    return jnp.dot(left, right, preferred_element_type=F32)


def left_mul(high_ref, low_ref, values):
    high, low = split(values)
    left = jnp.concatenate([high_ref[...], low_ref[...], high_ref[...]], axis=1)
    right = jnp.concatenate([high, high, low], axis=0)
    return jnp.dot(left, right, preferred_element_type=F32)


def forward_y(rows, tables):
    count = rows.shape[0] // 2
    half = rows.shape[1] // 2
    real, imag = rows[:count], rows[count:]
    even = jnp.concatenate(
        [real[:, :half] + real[:, half:], imag[:, :half] + imag[:, half:]], axis=1
    )
    odd = jnp.concatenate(
        [real[:, :half] - real[:, half:], imag[:, :half] - imag[:, half:]], axis=1
    )
    return jnp.concatenate(
        [right_mul(even, tables[0], tables[1]), right_mul(odd, tables[2], tables[3])], axis=1
    )


def store_send(send_ref, modes, field, field_count, plus, interleave):
    pieces = [modes[:, 128 * b : 128 * (b + 1)] for b in range(4)]
    if interleave:
        low_lane = lax.broadcasted_iota(jnp.int32, pieces[0].shape, 1) < 64
        out = []
        for b in range(2):
            even, odd = pieces[b], pieces[b + 2]
            out.append(jnp.where(low_lane, even, pltpu.roll(odd, 64, 1)))
            out.append(jnp.where(low_lane, pltpu.roll(even, 64, 1), odd))
        pieces = out
    phys = modes.shape[0] // plus
    chunk = send_ref.shape[1] // phys
    whole, rest = 8 * (plus // 8), plus % 8
    for owner in range(phys):
        parts = [(owner * whole, whole, 0), (phys * whole + owner * rest, rest, whole)]
        for start, size, first in parts:
            if not size:
                continue
            place = pl.ds(owner * chunk + first * field_count + field, size, stride=field_count)
            for b in range(4):
                send_ref[b, place, :] = pieces[b][start : start + size]


def rows_kernel(x_ref, fx_hi, fx_lo, out_ref):
    width = x_ref.shape[2]
    high, low = split(x_ref[...].reshape(-1, width))
    left = jnp.concatenate([fx_hi[...], fx_lo[...], fx_hi[...]], axis=1)
    right = jnp.concatenate([high, high, low], axis=1)
    rows = lax.dot_general(left, right, (((1,), (1,)), ((), ())), preferred_element_type=F32)
    for group in range(out_ref.shape[0]):
        out_ref[group] = rows[:, 128 * group : 128 * (group + 1)]


def swap_lanes(first, second, width):
    lane = lax.broadcasted_iota(jnp.int32, first.shape, 1)
    keep = (lane // width) % 2 == 0
    return (
        jnp.where(keep, first, pltpu.roll(second, width, 1)),
        jnp.where(keep, pltpu.roll(first, 128 - width, 1), second),
    )


def gather_rows(pieces):
    left = swap_lanes(pieces[0], pieces[2], 64)
    right = swap_lanes(pieces[1], pieces[3], 64)
    return swap_lanes(left[0], right[0], 32) + swap_lanes(left[1], right[1], 32)


def columns_kernel(
    interleave, field_count, plus, x_ref, e_hi, e_lo, o_hi, o_lo, s_ref, send_ref
):
    halves = [gather_rows([x_ref[4 * h + q, 0] for q in range(4)]) for h in range(2)]
    fields = [jnp.concatenate([halves[0][i], halves[1][i]], axis=1) for i in range(4)]
    count = fields[0].shape[0] // 2
    rows = jnp.concatenate([f[:count] for f in fields] + [f[count:] for f in fields], axis=0)
    modes = forward_y(rows, (e_hi, e_lo, o_hi, o_lo))
    for i in range(4):
        own = modes[i * count : (i + 1) * count]
        s_ref[i] = own
        store_send(send_ref, own, pl.program_id(0) * 4 + i, field_count, plus, interleave)


def spectrum_kernel(interleave, field_count, plus, x_ref, fx_hi, fx_lo, e_hi, e_lo, o_hi, o_lo, s_ref, send_ref):
    width = x_ref.shape[3]
    grid_field = x_ref[:, 0].reshape(width, width)
    high, low = split(grid_field)
    left = jnp.concatenate([fx_hi[...], fx_lo[...], fx_hi[...]], axis=1)
    right = jnp.concatenate([high, high, low], axis=1)
    rows = lax.dot_general(left, right, (((1,), (1,)), ((), ())), preferred_element_type=F32)
    modes = forward_y(rows, (e_hi, e_lo, o_hi, o_lo))
    s_ref[0] = modes
    store_send(send_ref, modes, pl.program_id(0), field_count, plus, interleave)


def advance_kernel(
    interleave,
    field_count,
    plus,
    dt_ref,
    s_ref,
    force_ref,
    wave_x_ref,
    wave_y_ref,
    fx_hi,
    fx_lo,
    e_hi,
    e_lo,
    o_hi,
    o_lo,
    bx_hi,
    bx_lo,
    bk_hi,
    bk_lo,
    ye_hi,
    ye_lo,
    yo_hi,
    yo_lo,
    send_ref,
):
    stack, count = s_ref.shape[:2]
    width = s_ref.shape[2] // 2
    half = width // 2
    wave_x, wave_y = wave_x_ref[...], wave_y_ref[...]
    wave_sq = wave_x * wave_x + wave_y * wave_y
    inverse_sq = jnp.where(wave_sq > 0, 1.0 / jnp.where(wave_sq > 0, wave_sq, 1.0), 0.0)
    damping = VISCOSITY * wave_sq

    def tendency(modes):
        both = jnp.concatenate([m * inverse_sq for m in modes] + modes, axis=0)
        even = right_mul(both[:, :width], ye_hi, ye_lo)
        odd = right_mul(both[:, width:], yo_hi, yo_lo)
        first, second = even + odd, even - odd

        def columns(row, block):
            rows = slice(row * count, (row + 1) * count)
            real = slice(2 * block * half, (2 * block + 1) * half)
            imag = slice((2 * block + 1) * half, (2 * block + 2) * half)
            return jnp.concatenate(
                [
                    jnp.concatenate([first[rows, real], second[rows, real]], axis=1),
                    jnp.concatenate([first[rows, imag], second[rows, imag]], axis=1),
                ],
                axis=0,
            )

        rows = []
        for i in range(stack):
            vel_x = left_mul(bx_hi, bx_lo, columns(i, 1))
            grad_x = left_mul(bk_hi, bk_lo, columns(stack + i, 0))
            total = vel_x * grad_x
            minus_vel_y = left_mul(bk_hi, bk_lo, columns(i, 0))
            grad_y = left_mul(bx_hi, bx_lo, columns(stack + i, 1))
            total = force_ref[...] - (total - minus_vel_y * grad_y)
            rows.append(left_mul(fx_hi, fx_lo, total))
        rows = jnp.concatenate([r[:count] for r in rows] + [r[count:] for r in rows], axis=0)
        out = forward_y(rows, (e_hi, e_lo, o_hi, o_lo))
        return [out[i * count : (i + 1) * count] - damping * modes[i] for i in range(stack)]

    step = dt_ref[0]
    spectra = [s_ref[i] for i in range(stack)]
    middle = [s + (0.5 * step) * t for s, t in zip(spectra, tendency(spectra))]
    second = tendency(middle)
    for i in range(stack):
        field = pl.program_id(0) * stack + i
        advanced = spectra[i] + step * second[i]
        store_send(send_ref, advanced, field, field_count, plus, interleave)


def angle_kernel(
    plus, field_count, samples, chunk, got_ref, mat_hi, mat_lo, last_ref, out_ref, rows_ref
):
    sources = got_ref.shape[0] // chunk
    lanes = got_ref.shape[1]
    modes = mat_hi.shape[1] // 2
    quarter = lanes // 4
    merged = samples * modes
    blocks = merged // 128
    turning = len(last_ref.shape) == 2
    for k in range(plus):
        cos_rows, sin_rows = [], []
        for s in range(samples):
            if field_count < samples:
                picks, table = range(field_count), s
            else:
                picks, table = range(s, field_count, samples), 0
            values = jnp.concatenate(
                [got_ref[pl.ds(k * field_count + f, sources, stride=chunk), :] for f in picks],
                axis=0,
            )
            result = left_mul(mat_hi.at[table], mat_lo.at[table], values)
            cos_rows.append(result[:modes])
            sin_rows.append(result[modes:])
        cosine = jnp.concatenate(cos_rows, axis=0).T
        sine = jnp.concatenate(sin_rows, axis=0).T
        for parity in range(2):
            row = parity * 2 * quarter
            near, far = slice(row, row + quarter), slice(row + quarter, row + 2 * quarter)
            real = cosine[near] + sine[far]
            imag = cosine[far] - sine[near]
            if turning:
                turn_cos, turn_sin = last_ref[0:1], last_ref[1:2]
                pair = (turn_sin * imag - turn_cos * real, -(turn_sin * real + turn_cos * imag))
            else:
                pair = (real, imag)
            for part in range(2):
                for b in range(blocks):
                    place = (k * 2 + part) * blocks + b
                    rows_ref[place, pl.ds(parity, quarter, stride=2), :] = pair[part][
                        :, 128 * b : 128 * (b + 1)
                    ]
        for part in range(2):
            place = (k * 2 + part) * blocks
            joined = jnp.concatenate([rows_ref[place + b] for b in range(blocks)], axis=1)
            out_ref[part, k] = joined if turning else joined + last_ref[part, k]


def cost(flops):
    return pl.CostEstimate(flops=int(flops), bytes_accessed=8 * 1024 * 1024, transcendentals=0)


def whole_spec(shape):
    zeros = (0,) * len(shape)
    return pl.BlockSpec(tuple(shape), lambda *_: zeros)


def local(tables, vorticity, forcing_mode, time_step, rotation):
    angle_local, samples, row_count, width = vorticity.shape
    phys = lax.axis_size("phys")
    ang = lax.axis_size("ang")
    angle_total = angle_local * ang
    group_fields = angle_local * samples
    field_count = -(-group_fields // phys)
    plus = tables["plus"]
    count = plus * phys
    chunk = -(-plus * field_count // 8) * 8
    block = width // ang
    interleave = block == 64

    forcing = forcing_mode[0].astype(F32)
    rows_global = jnp.arange(width, dtype=jnp.int32).astype(F32)
    force = (-forcing * jnp.cos(forcing * (2 * jnp.pi * rows_global / width)))[None, :]

    fields = vorticity.reshape(group_fields, row_count, width)
    fwd = list(tables["fwd_x"]) + list(tables["fwd_y"][0]) + list(tables["fwd_y"][1])
    fwd = [jnp.asarray(t) for t in fwd]
    inv = list(tables["inv_x"]) + list(tables["inv_kx"]) + list(tables["inv_y"][0]) + list(tables["inv_y"][1])
    inv = [jnp.asarray(t) for t in inv]
    params = pltpu.CompilerParams(
        dimension_semantics=("arbitrary",), vmem_limit_bytes=56 * 1024 * 1024
    )
    send_shape = (4, phys * chunk, 128)
    fixed = (interleave, field_count, plus)
    modes_shape = [
        jax.ShapeDtypeStruct((field_count, count, 2 * width), F32),
        jax.ShapeDtypeStruct(send_shape, F32),
    ]
    if row_count == 32 and phys == 8 and group_fields % 32 == 0:
        groups = field_count // 4
        fields = pl.pallas_call(
            rows_kernel,
            grid=(group_fields // 32,),
            in_specs=[pl.BlockSpec((32, row_count, width), lambda n: (n, 0, 0))]
            + [whole_spec(t.shape) for t in fwd[:2]],
            out_specs=pl.BlockSpec((8, 2 * count, 128), lambda n: (n, 0, 0)),
            out_shape=jax.ShapeDtypeStruct((group_fields // 4, 2 * count, 128), F32),
            compiler_params=params,
            name="rows",
        )(fields, *fwd[:2])
        fields = fields.reshape(phys, groups * 2 * count, 128)
        fields = lax.all_to_all(fields, "phys", split_axis=0, concat_axis=0, tiled=True)
        start_modes, start_send = pl.pallas_call(
            functools.partial(columns_kernel, *fixed),
            grid=(groups,),
            in_specs=[pl.BlockSpec((phys, 1, 2 * count, 128), lambda g: (0, g, 0, 0))]
            + [whole_spec(t.shape) for t in fwd[2:]],
            out_specs=[
                pl.BlockSpec((4, count, 2 * width), lambda g: (g, 0, 0)),
                whole_spec(send_shape),
            ],
            out_shape=modes_shape,
            compiler_params=params,
            name="columns",
        )(fields.reshape(phys, groups, 2 * count, 128), *fwd[2:])
    else:
        extra = field_count * phys - group_fields
        fields = jnp.pad(fields, ((0, extra), (0, 0), (0, 0)))
        fields = fields.reshape(phys, field_count, row_count, width)
        fields = lax.all_to_all(fields, "phys", split_axis=0, concat_axis=0, tiled=True)
        start_modes, start_send = pl.pallas_call(
            functools.partial(spectrum_kernel, *fixed),
            grid=(field_count,),
            in_specs=[pl.BlockSpec((phys, 1, row_count, width), lambda f: (0, f, 0, 0))]
            + [whole_spec(t.shape) for t in fwd],
            out_specs=[
                pl.BlockSpec((1, count, 2 * width), lambda f: (f, 0, 0)),
                whole_spec(send_shape),
            ],
            out_shape=modes_shape,
            compiler_params=params,
            name="spectrum",
        )(fields, *fwd)

    def exchange(send):
        rows = chunk
        if interleave:
            send = send.reshape(ang * phys, rows, 128)
        else:
            send = send.reshape(2, 2, phys, rows, 128 // block, block)
            send = send.transpose(1, 4, 2, 3, 0, 5).reshape(ang * phys, rows, 2 * block)
        got = lax.all_to_all(send, ("ang", "phys"), split_axis=0, concat_axis=0, tiled=True)
        return got.reshape(ang * phys * rows, 2 * block)

    start = exchange(start_send)

    stack = 4 if field_count % 4 == 0 else 1
    extra = [force, jnp.asarray(tables["wave_x"]), jnp.asarray(tables["wave_y"])]
    adv_send = pl.pallas_call(
        functools.partial(advance_kernel, *fixed),
        grid=(field_count // stack,),
        in_specs=[
            pl.BlockSpec(memory_space=pltpu.SMEM),
            pl.BlockSpec((stack, count, 2 * width), lambda f: (f, 0, 0)),
        ]
        + [whole_spec(t.shape) for t in extra + fwd + inv],
        out_specs=whole_spec(send_shape),
        out_shape=jax.ShapeDtypeStruct(send_shape, F32),
        cost_estimate=cost(field_count * 24 * count * 6 * width * width),
        compiler_params=params,
        name="advance",
    )(time_step, start_modes, *extra, *fwd, *inv)
    adv_send, start = lax.optimization_barrier((adv_send, start))
    advanced = exchange(adv_send)

    each = field_count // samples if field_count >= samples else field_count
    tables_s = 1 if field_count >= samples else samples
    index = np.arange(field_count)[:, None] + field_count * np.arange(phys)[None, :]
    index = np.broadcast_to(index[:, None, :], (field_count, ang, phys))
    first = np.arange(ang)[None, :, None] * angle_local + index // samples
    turn = 2.0 * math.pi / angle_total * np.mod(
        first[..., None] * np.arange(angle_total), angle_total
    )
    pair = np.concatenate([np.cos(turn), np.sin(turn)], axis=-1) / math.sqrt(angle_total)
    pair = np.where((index < group_fields)[..., None], pair, 0.0)
    matrix = []
    for s in range(tables_s):
        if tables_s == 1:
            rows = pair[::samples]
        else:
            rows = np.where((index % samples == s)[..., None], pair, 0.0)
        matrix.append(rows.reshape(each * ang * phys, 2 * angle_total).T)
    mat_hi, mat_lo = [jnp.asarray(t) for t in split_table(np.stack(matrix))]
    signed_angle = jnp.asarray(signed(np.arange(angle_total), angle_total).astype(np.float32))
    turns = jnp.stack(
        [
            jnp.tile(jnp.cos(signed_angle * rotation[0]), samples),
            jnp.tile(jnp.sin(signed_angle * rotation[0]), samples),
        ]
    )
    merged = samples * angle_total

    def to_angles(got, last):
        return pl.pallas_call(
            functools.partial(angle_kernel, plus, field_count, samples, chunk),
            in_specs=[pl.BlockSpec(memory_space=pltpu.VMEM)] * 4,
            out_specs=pl.BlockSpec(memory_space=pltpu.VMEM),
            out_shape=jax.ShapeDtypeStruct((2, plus, block, merged), F32),
            scratch_shapes=[pltpu.VMEM((plus * 2 * merged // 128, block, 128), F32)],
            cost_estimate=cost(2 * plus * 2 * block * 3 * mat_hi.shape[2] * 2 * merged),
            compiler_params=pltpu.CompilerParams(vmem_limit_bytes=40 * 1024 * 1024),
            name="angle",
        )(got, mat_hi, mat_lo, last)

    return to_angles(advanced, to_angles(start, turns))


def solution(mesh):
    in_specs = (P("ang", None, "phys", None), P(), P(), P())
    out_specs = P(None, "phys", "ang", None)

    def program(vorticity, forcing_mode, time_step, rotation):
        tables = make_tables(vorticity.shape[3], mesh.shape["phys"], mesh.shape["ang"])
        return jax.shard_map(
            functools.partial(local, tables),
            mesh=mesh,
            in_specs=in_specs,
            out_specs=out_specs,
            check_vma=False,
        )(vorticity, forcing_mode, time_step, rotation)

    return program
```

```python
import functools
import math

import jax
import jax.numpy as jnp
import ml_dtypes
import numpy as np
from jax import lax
from jax.experimental import pallas as pl
from jax.experimental.pallas import tpu as pltpu
from jax.sharding import PartitionSpec as P

VISCOSITY = 1.0 / 40.0
F32 = jnp.float32
BF16 = jnp.bfloat16


def split_table(table):
    table = np.asarray(table, np.float32)
    high = table.astype(ml_dtypes.bfloat16)
    low = (table - high.astype(np.float32)).astype(ml_dtypes.bfloat16)
    return high, low


def signed(values, length):
    return np.where(values < length // 2, values, values - length)


def make_tables(width, phys, ang):
    limit = width // 3
    half = width // 2
    plus = (limit + phys) // phys
    count = plus * phys
    full = 8 * phys * (plus // 8)
    row = np.arange(count)
    rest = plus % 8
    kx = np.where(
        row < full,
        (row % max(full, 1)) // 8 // max(plus // 8, 1) * plus + row % (8 * max(plus // 8, 1)),
        (row - full) // max(rest, 1) * plus + plus - rest + (row - full) % max(rest, 1),
    )
    kx_keep = (kx <= limit).astype(np.float64)
    block = width // ang
    lane = np.arange(width)
    owner = lane // block
    part = (lane % block) // (block // 2)
    even_index = owner * block + 2 * (lane % (block // 2))
    turn = 2.0 * math.pi / width
    grid = np.arange(width)

    def angle(left, right):
        return turn * np.mod(left[:, None] * right[None, :], width)

    x_turn = angle(kx, grid)
    fwd_x = np.concatenate([np.cos(x_turn), -np.sin(x_turn)]) / width
    fwd_x = fwd_x * np.concatenate([kx_keep, kx_keep])[:, None]
    weight = (np.where(kx == 0, 1.0, 2.0) * kx_keep)[:, None]
    inv_x = np.concatenate([weight * np.cos(x_turn), -weight * np.sin(x_turn)]).T
    inv_kx = np.concatenate(
        [-weight * kx[:, None] * np.sin(x_turn), -weight * kx[:, None] * np.cos(x_turn)]
    ).T
    fwd_y, inv_y, lane_ky = [], [], []
    for parity in (0, 1):
        ky = signed(even_index + parity, width)
        keep = (np.abs(ky) <= limit).astype(np.float64)
        lane_ky.append(ky)
        y_turn = angle(np.arange(half), ky)
        cos_y, sin_y = np.cos(y_turn) * keep, np.sin(y_turn) * keep
        real_out = part == 0
        from_real = np.where(real_out, cos_y, -sin_y)
        from_imag = np.where(real_out, sin_y, cos_y)
        fwd_y.append(np.concatenate([from_real, from_imag]) / width)
        real_back = np.where(real_out, cos_y, -sin_y).T
        imag_back = np.where(real_out, sin_y, cos_y).T
        scale = ky[:, None]
        inv_y.append(
            np.concatenate(
                [real_back, imag_back, -scale * imag_back, scale * real_back], axis=1
            )
        )
    return dict(
        plus=plus,
        fwd_x=split_table(fwd_x),
        inv_x=split_table(inv_x),
        inv_kx=split_table(inv_kx),
        fwd_y=[split_table(t) for t in fwd_y],
        inv_y=[split_table(t) for t in inv_y],
        wave_x=kx.astype(np.float32)[:, None],
        wave_y=np.concatenate(lane_ky).astype(np.float32)[None, :],
    )


def split(values):
    high = values.astype(BF16)
    low = (values - high.astype(F32)).astype(BF16)
    return high, low


def right_mul(values, high_ref, low_ref):
    high, low = split(values)
    left = jnp.concatenate([high, low, high], axis=1)
    right = jnp.concatenate([high_ref[...], high_ref[...], low_ref[...]], axis=0)
    return jnp.dot(left, right, preferred_element_type=F32)


def left_mul(high_ref, low_ref, values):
    high, low = split(values)
    left = jnp.concatenate([high_ref[...], low_ref[...], high_ref[...]], axis=1)
    right = jnp.concatenate([high, high, low], axis=0)
    return jnp.dot(left, right, preferred_element_type=F32)


def forward_y(rows, tables):
    count = rows.shape[0] // 2
    half = rows.shape[1] // 2
    real, imag = rows[:count], rows[count:]
    even = jnp.concatenate(
        [real[:, :half] + real[:, half:], imag[:, :half] + imag[:, half:]], axis=1
    )
    odd = jnp.concatenate(
        [real[:, :half] - real[:, half:], imag[:, :half] - imag[:, half:]], axis=1
    )
    return jnp.concatenate(
        [right_mul(even, tables[0], tables[1]), right_mul(odd, tables[2], tables[3])], axis=1
    )


def store_send(send_ref, modes, field, field_count, plus, interleave):
    pieces = [modes[:, 128 * b : 128 * (b + 1)] for b in range(4)]
    if interleave:
        low_lane = lax.broadcasted_iota(jnp.int32, pieces[0].shape, 1) < 64
        out = []
        for b in range(2):
            even, odd = pieces[b], pieces[b + 2]
            out.append(jnp.where(low_lane, even, pltpu.roll(odd, 64, 1)))
            out.append(jnp.where(low_lane, pltpu.roll(even, 64, 1), odd))
        pieces = out
    phys = modes.shape[0] // plus
    chunk = send_ref.shape[1] // phys
    whole, rest = 8 * (plus // 8), plus % 8
    for owner in range(phys):
        parts = [(owner * whole, whole, 0), (phys * whole + owner * rest, rest, whole)]
        for start, size, first in parts:
            if not size:
                continue
            place = pl.ds(owner * chunk + first * field_count + field, size, stride=field_count)
            for b in range(4):
                send_ref[b, place, :] = pieces[b][start : start + size]


def rows_kernel(x_ref, fx_hi, fx_lo, out_ref):
    width = x_ref.shape[2]
    high, low = split(x_ref[...].reshape(-1, width))
    left = jnp.concatenate([fx_hi[...], fx_lo[...], fx_hi[...]], axis=1)
    right = jnp.concatenate([high, high, low], axis=1)
    rows = lax.dot_general(left, right, (((1,), (1,)), ((), ())), preferred_element_type=F32)
    for group in range(out_ref.shape[0]):
        out_ref[group] = rows[:, 128 * group : 128 * (group + 1)]


def swap_lanes(first, second, width):
    lane = lax.broadcasted_iota(jnp.int32, first.shape, 1)
    keep = (lane // width) % 2 == 0
    return (
        jnp.where(keep, first, pltpu.roll(second, width, 1)),
        jnp.where(keep, pltpu.roll(first, 128 - width, 1), second),
    )


def gather_rows(pieces):
    left = swap_lanes(pieces[0], pieces[2], 64)
    right = swap_lanes(pieces[1], pieces[3], 64)
    return swap_lanes(left[0], right[0], 32) + swap_lanes(left[1], right[1], 32)


def four_modes(x_ref, e_hi, e_lo, o_hi, o_lo):
    halves = [gather_rows([x_ref[4 * h + q, 0] for q in range(4)]) for h in range(2)]
    fields = [jnp.concatenate([halves[0][i], halves[1][i]], axis=1) for i in range(4)]
    count = fields[0].shape[0] // 2
    rows = jnp.concatenate([f[:count] for f in fields] + [f[count:] for f in fields], axis=0)
    modes = forward_y(rows, (e_hi, e_lo, o_hi, o_lo))
    return [modes[i * count : (i + 1) * count] for i in range(4)]


def columns_kernel(interleave, field_count, plus, x_ref, e_hi, e_lo, o_hi, o_lo, send_ref):
    modes = four_modes(x_ref, e_hi, e_lo, o_hi, o_lo)
    for i in range(4):
        field = pl.program_id(0) * 4 + i
        store_send(send_ref, modes[i], field, field_count, plus, interleave)


def spectrum_kernel(interleave, field_count, plus, x_ref, fx_hi, fx_lo, e_hi, e_lo, o_hi, o_lo, s_ref, send_ref):
    width = x_ref.shape[3]
    grid_field = x_ref[:, 0].reshape(width, width)
    high, low = split(grid_field)
    left = jnp.concatenate([fx_hi[...], fx_lo[...], fx_hi[...]], axis=1)
    right = jnp.concatenate([high, high, low], axis=1)
    rows = lax.dot_general(left, right, (((1,), (1,)), ((), ())), preferred_element_type=F32)
    modes = forward_y(rows, (e_hi, e_lo, o_hi, o_lo))
    s_ref[0] = modes
    store_send(send_ref, modes, pl.program_id(0), field_count, plus, interleave)


def advance_kernel(
    interleave,
    field_count,
    plus,
    dt_ref,
    s_ref,
    force_ref,
    wave_x_ref,
    wave_y_ref,
    fx_hi,
    fx_lo,
    e_hi,
    e_lo,
    o_hi,
    o_lo,
    bx_hi,
    bx_lo,
    bk_hi,
    bk_lo,
    ye_hi,
    ye_lo,
    yo_hi,
    yo_lo,
    send_ref,
):
    if len(s_ref.shape) == 4:
        spectra = four_modes(s_ref, e_hi, e_lo, o_hi, o_lo)
    else:
        spectra = [s_ref[i] for i in range(s_ref.shape[0])]
    stack = len(spectra)
    count, width = spectra[0].shape[0], spectra[0].shape[1] // 2
    half = width // 2
    wave_x, wave_y = wave_x_ref[...], wave_y_ref[...]
    wave_sq = wave_x * wave_x + wave_y * wave_y
    inverse_sq = jnp.where(wave_sq > 0, 1.0 / jnp.where(wave_sq > 0, wave_sq, 1.0), 0.0)
    damping = VISCOSITY * wave_sq

    def tendency(modes):
        both = jnp.concatenate([m * inverse_sq for m in modes] + modes, axis=0)
        even = right_mul(both[:, :width], ye_hi, ye_lo)
        odd = right_mul(both[:, width:], yo_hi, yo_lo)
        first, second = even + odd, even - odd

        def columns(row, block):
            rows = slice(row * count, (row + 1) * count)
            real = slice(2 * block * half, (2 * block + 1) * half)
            imag = slice((2 * block + 1) * half, (2 * block + 2) * half)
            return jnp.concatenate(
                [
                    jnp.concatenate([first[rows, real], second[rows, real]], axis=1),
                    jnp.concatenate([first[rows, imag], second[rows, imag]], axis=1),
                ],
                axis=0,
            )

        rows = []
        for i in range(stack):
            vel_x = left_mul(bx_hi, bx_lo, columns(i, 1))
            grad_x = left_mul(bk_hi, bk_lo, columns(stack + i, 0))
            total = vel_x * grad_x
            minus_vel_y = left_mul(bk_hi, bk_lo, columns(i, 0))
            grad_y = left_mul(bx_hi, bx_lo, columns(stack + i, 1))
            total = force_ref[...] - (total - minus_vel_y * grad_y)
            rows.append(left_mul(fx_hi, fx_lo, total))
        rows = jnp.concatenate([r[:count] for r in rows] + [r[count:] for r in rows], axis=0)
        out = forward_y(rows, (e_hi, e_lo, o_hi, o_lo))
        return [out[i * count : (i + 1) * count] - damping * modes[i] for i in range(stack)]

    step = dt_ref[0]
    middle = [s + (0.5 * step) * t for s, t in zip(spectra, tendency(spectra))]
    second = tendency(middle)
    for i in range(stack):
        field = pl.program_id(0) * stack + i
        advanced = spectra[i] + step * second[i]
        store_send(send_ref, advanced, field, field_count, plus, interleave)


def angle_kernel(
    plus,
    field_count,
    samples,
    turning,
    got_hbm,
    mat_hi,
    mat_lo,
    last_ref,
    out_hbm,
    got_ref,
    last_buf,
    out_buf,
    rows_ref,
    got_sem,
    last_sem,
    out_sem,
):
    sources, chunk, lanes = got_hbm.shape
    modes = mat_hi.shape[1] // 2
    quarter = lanes // 4
    merged = samples * modes
    blocks = merged // 128
    parts = input_parts(plus, field_count, chunk)
    loads = []
    for n, (first_k, first, size) in enumerate(parts):
        place = (slice(None), slice(first, first + size))
        copies = [pltpu.make_async_copy(got_hbm.at[place], got_ref.at[place], got_sem.at[n])]
        if not turning:
            last_k = parts[n + 1][0] if n + 1 < len(parts) else plus
            place = (slice(None), slice(first_k, last_k))
            copies.append(
                pltpu.make_async_copy(last_ref.at[place], last_buf.at[place], last_sem.at[n])
            )
        for copy in copies:
            copy.start()
        loads.append((first_k, copies))
    flat = got_ref.reshape(sources * chunk, lanes)
    stores = []
    for k in range(plus):
        for first_k, copies in loads:
            if first_k == k:
                for copy in copies:
                    copy.wait()
        cos_rows, sin_rows = [], []
        for s in range(samples):
            if field_count < samples:
                picks, table = range(field_count), s
            else:
                picks, table = range(s, field_count, samples), 0
            values = jnp.concatenate(
                [flat[pl.ds(k * field_count + f, sources, stride=chunk), :] for f in picks],
                axis=0,
            )
            result = left_mul(mat_hi.at[table], mat_lo.at[table], values)
            cos_rows.append(result[:modes])
            sin_rows.append(result[modes:])
        cosine = jnp.concatenate(cos_rows, axis=0).T
        sine = jnp.concatenate(sin_rows, axis=0).T
        for parity in range(2):
            row = parity * 2 * quarter
            near, far = slice(row, row + quarter), slice(row + quarter, row + 2 * quarter)
            real = cosine[near] + sine[far]
            imag = cosine[far] - sine[near]
            if turning:
                turn_cos, turn_sin = last_ref[0:1], last_ref[1:2]
                pair = (turn_sin * imag - turn_cos * real, -(turn_sin * real + turn_cos * imag))
            else:
                pair = (real, imag)
            for part in range(2):
                for b in range(blocks):
                    place = (k * 2 + part) * blocks + b
                    rows_ref[place, pl.ds(parity, quarter, stride=2), :] = pair[part][
                        :, 128 * b : 128 * (b + 1)
                    ]
        for part in range(2):
            place = (k * 2 + part) * blocks
            joined = jnp.concatenate([rows_ref[place + b] for b in range(blocks)], axis=1)
            out_buf[part, k] = joined if turning else joined + last_buf[part, k]
        copy = pltpu.make_async_copy(out_buf.at[:, k], out_hbm.at[:, k], out_sem.at[k])
        copy.start()
        stores.append(copy)
    for copy in stores:
        copy.wait()


def input_parts(plus, field_count, chunk):
    cuts = [k for k in range(1, plus) if k % 4 == 0 and k * field_count % 8 == 0]
    firsts = [0] + cuts
    rows = [k * field_count for k in firsts] + [chunk]
    return [(k, rows[n], rows[n + 1] - rows[n]) for n, k in enumerate(firsts)]


def cost(flops):
    return pl.CostEstimate(flops=int(flops), bytes_accessed=8 * 1024 * 1024, transcendentals=0)


def in_hbm(values):
    return pltpu.with_memory_space_constraint(values, pltpu.HBM)


def whole_spec(shape):
    zeros = (0,) * len(shape)
    return pl.BlockSpec(tuple(shape), lambda *_: zeros)


def local(tables, vorticity, forcing_mode, time_step, rotation):
    angle_local, samples, row_count, width = vorticity.shape
    phys = lax.axis_size("phys")
    ang = lax.axis_size("ang")
    angle_total = angle_local * ang
    group_fields = angle_local * samples
    field_count = -(-group_fields // phys)
    plus = tables["plus"]
    count = plus * phys
    chunk = -(-plus * field_count // 8) * 8
    block = width // ang
    interleave = block == 64

    forcing = forcing_mode[0].astype(F32)
    rows_global = jnp.arange(width, dtype=jnp.int32).astype(F32)
    force = (-forcing * jnp.cos(forcing * (2 * jnp.pi * rows_global / width)))[None, :]

    fields = vorticity.reshape(group_fields, row_count, width)
    fwd = list(tables["fwd_x"]) + list(tables["fwd_y"][0]) + list(tables["fwd_y"][1])
    fwd = [jnp.asarray(t) for t in fwd]
    inv = list(tables["inv_x"]) + list(tables["inv_kx"]) + list(tables["inv_y"][0]) + list(tables["inv_y"][1])
    inv = [in_hbm(jnp.asarray(t)) for t in inv]
    def params(megabytes):
        return pltpu.CompilerParams(
            dimension_semantics=("arbitrary",), vmem_limit_bytes=megabytes * 1024 * 1024
        )

    send_shape = (4, phys * chunk, 128)
    fixed = (interleave, field_count, plus)
    send_out = pltpu.HBM(send_shape, F32)
    if row_count == 32 and phys == 8 and group_fields % 32 == 0:
        groups = field_count // 4
        fields = pl.pallas_call(
            rows_kernel,
            grid=(group_fields // 32,),
            in_specs=[pl.BlockSpec((32, row_count, width), lambda n: (n, 0, 0))]
            + [whole_spec(t.shape) for t in fwd[:2]],
            out_specs=pl.BlockSpec((8, 2 * count, 128), lambda n: (n, 0, 0)),
            out_shape=jax.ShapeDtypeStruct((group_fields // 4, 2 * count, 128), F32),
            compiler_params=params(20),
            name="rows",
        )(in_hbm(fields), *map(in_hbm, fwd[:2]))
        fields = fields.reshape(phys, groups * 2 * count, 128)
        fields = lax.all_to_all(fields, "phys", split_axis=0, concat_axis=0, tiled=True)
        spectra = fields.reshape(phys, groups, 2 * count, 128)
        spectra_spec = pl.BlockSpec((phys, 1, 2 * count, 128), lambda g: (0, g, 0, 0))
        start_send = pl.pallas_call(
            functools.partial(columns_kernel, *fixed),
            grid=(groups,),
            in_specs=[spectra_spec] + [whole_spec(t.shape) for t in fwd[2:]],
            out_specs=whole_spec(send_shape),
            out_shape=jax.ShapeDtypeStruct(send_shape, F32),
            compiler_params=params(20),
            name="columns",
        )(spectra, *fwd[2:])
        stack = 4
    else:
        extra = field_count * phys - group_fields
        fields = jnp.pad(fields, ((0, extra), (0, 0), (0, 0)))
        fields = fields.reshape(phys, field_count, row_count, width)
        fields = lax.all_to_all(fields, "phys", split_axis=0, concat_axis=0, tiled=True)
        spectra, start_send = pl.pallas_call(
            functools.partial(spectrum_kernel, *fixed),
            grid=(field_count,),
            in_specs=[pl.BlockSpec((phys, 1, row_count, width), lambda f: (0, f, 0, 0))]
            + [whole_spec(t.shape) for t in fwd],
            out_specs=[
                pl.BlockSpec((1, count, 2 * width), lambda f: (f, 0, 0)),
                whole_spec(send_shape),
            ],
            out_shape=[
                jax.ShapeDtypeStruct((field_count, count, 2 * width), F32),
                jax.ShapeDtypeStruct(send_shape, F32),
            ],
            compiler_params=params(24),
            name="spectrum",
        )(fields, *fwd)
        spectra_spec = pl.BlockSpec((1, count, 2 * width), lambda f: (f, 0, 0))
        stack = 1

    def exchange(send):
        rows = chunk
        if interleave:
            send = send.reshape(ang * phys, rows, 128)
        else:
            send = send.reshape(2, 2, phys, rows, 128 // block, block)
            send = send.transpose(1, 4, 2, 3, 0, 5).reshape(ang * phys, rows, 2 * block)
        got = lax.all_to_all(send, ("ang", "phys"), split_axis=0, concat_axis=0, tiled=True)
        return got

    start = exchange(start_send)

    extra = [force, jnp.asarray(tables["wave_x"]), jnp.asarray(tables["wave_y"])]
    adv_send = pl.pallas_call(
        functools.partial(advance_kernel, *fixed),
        grid=(field_count // stack,),
        in_specs=[
            pl.BlockSpec(memory_space=pltpu.SMEM),
            spectra_spec,
        ]
        + [whole_spec(t.shape) for t in extra + fwd + inv],
        out_specs=whole_spec(send_shape),
        out_shape=send_out,
        cost_estimate=cost(field_count * 24 * count * 6 * width * width),
        compiler_params=params(36),
        name="advance",
    )(time_step, spectra, *extra, *map(in_hbm, fwd), *inv)
    adv_send, start = lax.optimization_barrier((adv_send, start))
    advanced = exchange(adv_send)

    each = field_count // samples if field_count >= samples else field_count
    tables_s = 1 if field_count >= samples else samples
    index = np.arange(field_count)[:, None] + field_count * np.arange(phys)[None, :]
    index = np.broadcast_to(index[:, None, :], (field_count, ang, phys))
    first = np.arange(ang)[None, :, None] * angle_local + index // samples
    turn = 2.0 * math.pi / angle_total * np.mod(
        first[..., None] * np.arange(angle_total), angle_total
    )
    pair = np.concatenate([np.cos(turn), np.sin(turn)], axis=-1) / math.sqrt(angle_total)
    pair = np.where((index < group_fields)[..., None], pair, 0.0)
    matrix = []
    for s in range(tables_s):
        if tables_s == 1:
            rows = pair[::samples]
        else:
            rows = np.where((index % samples == s)[..., None], pair, 0.0)
        matrix.append(rows.reshape(each * ang * phys, 2 * angle_total).T)
    mat_hi, mat_lo = [jnp.asarray(t) for t in split_table(np.stack(matrix))]
    signed_angle = jnp.asarray(signed(np.arange(angle_total), angle_total).astype(np.float32))
    turns = jnp.stack(
        [
            jnp.tile(jnp.cos(signed_angle * rotation[0]), samples),
            jnp.tile(jnp.sin(signed_angle * rotation[0]), samples),
        ]
    )
    merged = samples * angle_total

    parts = len(input_parts(plus, field_count, chunk))
    out_shape = (2, plus, block, merged)
    vmem = pl.BlockSpec(memory_space=pltpu.VMEM)
    hbm = pl.BlockSpec(memory_space=pltpu.HBM)

    def to_angles(got, last, turning):
        return pl.pallas_call(
            functools.partial(angle_kernel, plus, field_count, samples, turning),
            in_specs=[hbm, vmem, vmem, vmem if turning else hbm],
            out_specs=hbm,
            out_shape=pltpu.HBM(out_shape, F32),
            scratch_shapes=[
                pltpu.VMEM(got.shape, F32),
                pltpu.VMEM((8, 128) if turning else out_shape, F32),
                pltpu.VMEM(out_shape, F32),
                pltpu.VMEM((plus * 2 * merged // 128, block, 128), F32),
                pltpu.SemaphoreType.DMA((parts,)),
                pltpu.SemaphoreType.DMA((parts,)),
                pltpu.SemaphoreType.DMA((plus,)),
            ],
            cost_estimate=cost(2 * plus * 2 * block * 3 * mat_hi.shape[2] * 2 * merged),
            compiler_params=pltpu.CompilerParams(vmem_limit_bytes=20 * 1024 * 1024),
            name="angle",
        )(got, mat_hi, mat_lo, last)

    start_part = in_hbm(to_angles(start, turns, True))
    return to_angles(advanced, start_part, False)


def solution(mesh):
    in_specs = (P("ang", None, "phys", None), P(), P(), P())
    out_specs = P(None, "phys", "ang", None)

    def program(vorticity, forcing_mode, time_step, rotation):
        tables = make_tables(vorticity.shape[3], mesh.shape["phys"], mesh.shape["ang"])
        return jax.shard_map(
            functools.partial(local, tables),
            mesh=mesh,
            in_specs=in_specs,
            out_specs=out_specs,
            check_vma=False,
        )(vorticity, forcing_mode, time_step, rotation)

    return program
```

```python
import functools
import math

import jax
import jax.numpy as jnp
import ml_dtypes
import numpy as np
from jax import lax
from jax.experimental import pallas as pl
from jax.experimental.pallas import tpu as pltpu
from jax.sharding import PartitionSpec as P

VISCOSITY = 1.0 / 40.0
F32 = jnp.float32
BF16 = jnp.bfloat16


def split_table(table):
    table = np.asarray(table, np.float32)
    high = table.astype(ml_dtypes.bfloat16)
    low = (table - high.astype(np.float32)).astype(ml_dtypes.bfloat16)
    return high, low


def signed(values, length):
    return np.where(values < length // 2, values, values - length)


def make_tables(width, phys, ang):
    limit = width // 3
    half = width // 2
    plus = (limit + phys) // phys
    count = plus * phys
    full = 8 * phys * (plus // 8)
    row = np.arange(count)
    rest = plus % 8
    kx = np.where(
        row < full,
        (row % max(full, 1)) // 8 // max(plus // 8, 1) * plus + row % (8 * max(plus // 8, 1)),
        (row - full) // max(rest, 1) * plus + plus - rest + (row - full) % max(rest, 1),
    )
    kx_keep = (kx <= limit).astype(np.float64)
    block = width // ang
    lane = np.arange(width)
    owner = lane // block
    part = (lane % block) // (block // 2)
    even_index = owner * block + 2 * (lane % (block // 2))
    turn = 2.0 * math.pi / width
    grid = np.arange(width)

    def angle(left, right):
        return turn * np.mod(left[:, None] * right[None, :], width)

    x_turn = angle(kx, grid)
    fwd_x = np.concatenate([np.cos(x_turn), -np.sin(x_turn)]) / width
    fwd_x = fwd_x * np.concatenate([kx_keep, kx_keep])[:, None]
    weight = (np.where(kx == 0, 1.0, 2.0) * kx_keep)[:, None]
    inv_x = np.concatenate([weight * np.cos(x_turn), -weight * np.sin(x_turn)]).T
    inv_kx = np.concatenate(
        [-weight * kx[:, None] * np.sin(x_turn), -weight * kx[:, None] * np.cos(x_turn)]
    ).T
    fwd_y, inv_y, lane_ky = [], [], []
    for parity in (0, 1):
        ky = signed(even_index + parity, width)
        keep = (np.abs(ky) <= limit).astype(np.float64)
        lane_ky.append(ky)
        y_turn = angle(np.arange(half), ky)
        cos_y, sin_y = np.cos(y_turn) * keep, np.sin(y_turn) * keep
        real_out = part == 0
        from_real = np.where(real_out, cos_y, -sin_y)
        from_imag = np.where(real_out, sin_y, cos_y)
        fwd_y.append(np.concatenate([from_real, from_imag]) / width)
        real_back = np.where(real_out, cos_y, -sin_y).T
        imag_back = np.where(real_out, sin_y, cos_y).T
        scale = ky[:, None]
        inv_y.append(
            np.concatenate(
                [real_back, imag_back, -scale * imag_back, scale * real_back], axis=1
            )
        )
    return dict(
        plus=plus,
        fwd_x=split_table(fwd_x),
        inv_x=split_table(inv_x),
        inv_kx=split_table(inv_kx),
        fwd_y=[split_table(t) for t in fwd_y],
        inv_y=[split_table(t) for t in inv_y],
        wave_x=kx.astype(np.float32)[:, None],
        wave_y=np.concatenate(lane_ky).astype(np.float32)[None, :],
    )


def split(values):
    high = values.astype(BF16)
    low = (values - high.astype(F32)).astype(BF16)
    return high, low


def right_mul(values, high_ref, low_ref):
    high, low = split(values)
    left = jnp.concatenate([high, low, high], axis=1)
    right = jnp.concatenate([high_ref[...], high_ref[...], low_ref[...]], axis=0)
    return jnp.dot(left, right, preferred_element_type=F32)


def left_mul(high_ref, low_ref, values):
    high, low = split(values)
    left = jnp.concatenate([high_ref[...], low_ref[...], high_ref[...]], axis=1)
    right = jnp.concatenate([high, high, low], axis=0)
    return jnp.dot(left, right, preferred_element_type=F32)


def forward_y(rows, tables):
    count = rows.shape[0] // 2
    half = rows.shape[1] // 2
    real, imag = rows[:count], rows[count:]
    even = jnp.concatenate(
        [real[:, :half] + real[:, half:], imag[:, :half] + imag[:, half:]], axis=1
    )
    odd = jnp.concatenate(
        [real[:, :half] - real[:, half:], imag[:, :half] - imag[:, half:]], axis=1
    )
    return jnp.concatenate(
        [right_mul(even, tables[0], tables[1]), right_mul(odd, tables[2], tables[3])], axis=1
    )


def store_send(send_ref, modes, field, field_count, plus, interleave):
    pieces = [modes[:, 128 * b : 128 * (b + 1)] for b in range(4)]
    if interleave:
        low_lane = lax.broadcasted_iota(jnp.int32, pieces[0].shape, 1) < 64
        out = []
        for b in range(2):
            even, odd = pieces[b], pieces[b + 2]
            out.append(jnp.where(low_lane, even, pltpu.roll(odd, 64, 1)))
            out.append(jnp.where(low_lane, pltpu.roll(even, 64, 1), odd))
        pieces = out
    phys = modes.shape[0] // plus
    chunk = send_ref.shape[1] // phys
    if chunk < plus * field_count:
        store_levelled(send_ref, pieces, field, field_count)
        return
    whole, rest = 8 * (plus // 8), plus % 8
    for owner in range(phys):
        parts = [(owner * whole, whole, 0), (phys * whole + owner * rest, rest, whole)]
        for start, size, first in parts:
            if not size:
                continue
            place = pl.ds(owner * chunk + first * field_count + field, size, stride=field_count)
            for b in range(4):
                send_ref[b, place, :] = pieces[b][start : start + size]


def store_levelled(send_ref, pieces, field, field_count):
    phys = 8
    chunk = send_ref.shape[1] // phys
    lane = lax.broadcasted_iota(jnp.int32, pieces[0].shape, 1)
    low = lane % 32 < 16

    def pair(values, other, upper):
        if upper:
            return jnp.where(low, pltpu.roll(values, 128 - 16, 1), other)
        return jnp.where(low, values, pltpu.roll(other, 16, 1))

    def put(owner, p, unit, rows):
        place = pl.ds(p * chunk + unit * field_count + field, rows.shape[0], stride=field_count)
        send_ref[owner, place, :] = rows

    count = pieces[0].shape[0]
    for end, middle in ((0, 1), (3, 2)):
        whole, part = pieces[end], pieces[middle]
        fours = pair(part, pltpu.roll(part, count - 4, 0), middle == 2)
        ones = pair(part, pltpu.roll(part, count - 1, 0), middle == 2)
        for p in range(phys):
            tail = 64 + 3 * p
            put(end, p, 0, whole[8 * p : 8 * p + 8])
            put(end, p, 8, whole[tail : tail + 1])
            put(middle, p, 0, whole[tail + 1 : tail + 3])
            put(middle, p, 2, fours[8 * p : 8 * p + 4])
            put(middle, p, 6, ones[tail : tail + 1])
            put(middle, p, 7, ones[tail + 2 : tail + 3])


def rows_kernel(x_ref, fx_hi, fx_lo, out_ref):
    width = x_ref.shape[2]
    high, low = split(x_ref[...].reshape(-1, width))
    left = jnp.concatenate([fx_hi[...], fx_lo[...], fx_hi[...]], axis=1)
    right = jnp.concatenate([high, high, low], axis=1)
    rows = lax.dot_general(left, right, (((1,), (1,)), ((), ())), preferred_element_type=F32)
    for group in range(out_ref.shape[0]):
        out_ref[group] = rows[:, 128 * group : 128 * (group + 1)]


def swap_lanes(first, second, width):
    lane = lax.broadcasted_iota(jnp.int32, first.shape, 1)
    keep = (lane // width) % 2 == 0
    return (
        jnp.where(keep, first, pltpu.roll(second, width, 1)),
        jnp.where(keep, pltpu.roll(first, 128 - width, 1), second),
    )


def gather_rows(pieces):
    left = swap_lanes(pieces[0], pieces[2], 64)
    right = swap_lanes(pieces[1], pieces[3], 64)
    return swap_lanes(left[0], right[0], 32) + swap_lanes(left[1], right[1], 32)


def four_modes(x_ref, e_hi, e_lo, o_hi, o_lo):
    halves = [gather_rows([x_ref[4 * h + q, 0] for q in range(4)]) for h in range(2)]
    fields = [jnp.concatenate([halves[0][i], halves[1][i]], axis=1) for i in range(4)]
    count = fields[0].shape[0] // 2
    rows = jnp.concatenate([f[:count] for f in fields] + [f[count:] for f in fields], axis=0)
    modes = forward_y(rows, (e_hi, e_lo, o_hi, o_lo))
    return [modes[i * count : (i + 1) * count] for i in range(4)]


def columns_kernel(interleave, field_count, plus, x_ref, e_hi, e_lo, o_hi, o_lo, send_ref):
    modes = four_modes(x_ref, e_hi, e_lo, o_hi, o_lo)
    for i in range(4):
        field = pl.program_id(0) * 4 + i
        store_send(send_ref, modes[i], field, field_count, plus, interleave)


def spectrum_kernel(interleave, field_count, plus, x_ref, fx_hi, fx_lo, e_hi, e_lo, o_hi, o_lo, s_ref, send_ref):
    width = x_ref.shape[3]
    grid_field = x_ref[:, 0].reshape(width, width)
    high, low = split(grid_field)
    left = jnp.concatenate([fx_hi[...], fx_lo[...], fx_hi[...]], axis=1)
    right = jnp.concatenate([high, high, low], axis=1)
    rows = lax.dot_general(left, right, (((1,), (1,)), ((), ())), preferred_element_type=F32)
    modes = forward_y(rows, (e_hi, e_lo, o_hi, o_lo))
    s_ref[0] = modes
    store_send(send_ref, modes, pl.program_id(0), field_count, plus, interleave)


def advance_kernel(
    interleave,
    field_count,
    plus,
    dt_ref,
    s_ref,
    force_ref,
    wave_x_ref,
    wave_y_ref,
    fx_hi,
    fx_lo,
    e_hi,
    e_lo,
    o_hi,
    o_lo,
    bx_hi,
    bx_lo,
    bk_hi,
    bk_lo,
    ye_hi,
    ye_lo,
    yo_hi,
    yo_lo,
    send_ref,
):
    if len(s_ref.shape) == 4:
        spectra = four_modes(s_ref, e_hi, e_lo, o_hi, o_lo)
    else:
        spectra = [s_ref[i] for i in range(s_ref.shape[0])]
    stack = len(spectra)
    count, width = spectra[0].shape[0], spectra[0].shape[1] // 2
    half = width // 2
    wave_x, wave_y = wave_x_ref[...], wave_y_ref[...]
    wave_sq = wave_x * wave_x + wave_y * wave_y
    inverse_sq = jnp.where(wave_sq > 0, 1.0 / jnp.where(wave_sq > 0, wave_sq, 1.0), 0.0)
    damping = VISCOSITY * wave_sq

    def tendency(modes):
        both = jnp.concatenate([m * inverse_sq for m in modes] + modes, axis=0)
        even = right_mul(both[:, :width], ye_hi, ye_lo)
        odd = right_mul(both[:, width:], yo_hi, yo_lo)
        first, second = even + odd, even - odd

        def columns(row, block):
            rows = slice(row * count, (row + 1) * count)
            real = slice(2 * block * half, (2 * block + 1) * half)
            imag = slice((2 * block + 1) * half, (2 * block + 2) * half)
            return jnp.concatenate(
                [
                    jnp.concatenate([first[rows, real], second[rows, real]], axis=1),
                    jnp.concatenate([first[rows, imag], second[rows, imag]], axis=1),
                ],
                axis=0,
            )

        rows = []
        for i in range(stack):
            vel_x = left_mul(bx_hi, bx_lo, columns(i, 1))
            grad_x = left_mul(bk_hi, bk_lo, columns(stack + i, 0))
            total = vel_x * grad_x
            minus_vel_y = left_mul(bk_hi, bk_lo, columns(i, 0))
            grad_y = left_mul(bx_hi, bx_lo, columns(stack + i, 1))
            total = force_ref[...] - (total - minus_vel_y * grad_y)
            rows.append(left_mul(fx_hi, fx_lo, total))
        rows = jnp.concatenate([r[:count] for r in rows] + [r[count:] for r in rows], axis=0)
        out = forward_y(rows, (e_hi, e_lo, o_hi, o_lo))
        return [out[i * count : (i + 1) * count] - damping * modes[i] for i in range(stack)]

    step = dt_ref[0]
    middle = [s + (0.5 * step) * t for s, t in zip(spectra, tendency(spectra))]
    second = tendency(middle)
    for i in range(stack):
        field = pl.program_id(0) * stack + i
        advanced = spectra[i] + step * second[i]
        store_send(send_ref, advanced, field, field_count, plus, interleave)


def angle_kernel(
    plus,
    field_count,
    samples,
    turning,
    got_hbm,
    mat_hi,
    mat_lo,
    last_ref,
    out_hbm,
    got_ref,
    last_buf,
    out_buf,
    rows_ref,
    got_sem,
    last_sem,
    out_sem,
):
    sources, chunk, lanes = got_hbm.shape
    modes = mat_hi.shape[1] // 2
    quarter = lanes // 4
    merged = samples * modes
    blocks = merged // 128
    parts = input_parts(plus, field_count, chunk)
    loads = []
    for n, (first_k, first, size) in enumerate(parts):
        place = (slice(None), slice(first, first + size))
        copies = [pltpu.make_async_copy(got_hbm.at[place], got_ref.at[place], got_sem.at[n])]
        if not turning:
            last_k = parts[n + 1][0] if n + 1 < len(parts) else plus
            place = (slice(None), slice(first_k, last_k))
            copies.append(
                pltpu.make_async_copy(last_ref.at[place], last_buf.at[place], last_sem.at[n])
            )
        for copy in copies:
            copy.start()
        loads.append((first_k, copies))
    flat = got_ref.reshape(sources * chunk, lanes)
    stores = []
    for k in range(plus):
        for first_k, copies in loads:
            if first_k == k:
                for copy in copies:
                    copy.wait()
        cos_rows, sin_rows = [], []
        for s in range(samples):
            if field_count < samples:
                picks, table = range(field_count), s
            else:
                picks, table = range(s, field_count, samples), 0
            values = jnp.concatenate(
                [flat[pl.ds(k * field_count + f, sources, stride=chunk), :] for f in picks],
                axis=0,
            )
            result = left_mul(mat_hi.at[table], mat_lo.at[table], values)
            cos_rows.append(result[:modes])
            sin_rows.append(result[modes:])
        cosine = jnp.concatenate(cos_rows, axis=0).T
        sine = jnp.concatenate(sin_rows, axis=0).T
        for parity in range(2):
            row = parity * 2 * quarter
            near, far = slice(row, row + quarter), slice(row + quarter, row + 2 * quarter)
            real = cosine[near] + sine[far]
            imag = cosine[far] - sine[near]
            if turning:
                turn_cos, turn_sin = last_ref[0:1], last_ref[1:2]
                pair = (turn_sin * imag - turn_cos * real, -(turn_sin * real + turn_cos * imag))
            else:
                pair = (real, imag)
            for part in range(2):
                for b in range(blocks):
                    place = (k * 2 + part) * blocks + b
                    rows_ref[place, pl.ds(parity, quarter, stride=2), :] = pair[part][
                        :, 128 * b : 128 * (b + 1)
                    ]
        for part in range(2):
            place = (k * 2 + part) * blocks
            joined = jnp.concatenate([rows_ref[place + b] for b in range(blocks)], axis=1)
            out_buf[part, k] = joined if turning else joined + last_buf[part, k]
        if out_hbm is not None:
            copy = pltpu.make_async_copy(out_buf.at[:, k], out_hbm.at[:, k], out_sem.at[k])
            copy.start()
            stores.append(copy)
    for copy in stores:
        copy.wait()


def place_kernel(field_count, samples, kind_ref, got_hbm, mat_hi, mat_lo, last_ref, out_ref, *scratch):
    kind = kind_ref[0]
    result_buf = scratch[2]
    units = result_buf.shape[1]
    angle_kernel(
        units, field_count, samples, False, got_hbm, mat_hi, mat_lo, last_ref, None, *scratch
    )
    half = out_ref.shape[2] // 2
    zeros = jnp.zeros((2, 1) + out_ref.shape[2:], F32)

    @pl.when(kind == 0)
    def _():
        out_ref[:, :units] = result_buf[...]
        for k in range(units, out_ref.shape[1]):
            out_ref[:, k : k + 1] = zeros

    @pl.when(kind > 0)
    def _():
        first = pl.multiple_of((kind - 1) * half, half)
        other = pl.multiple_of(half - first, half)
        pairs = [(2 + k, 0, k) for k in range(4)] + [(2 + k, 1, 4 + k) for k in range(4)]
        pairs += [(6, 0, 8), (6, 1, 9), (7, 0, 10)]
        for unit, which, k in pairs:
            rows = result_buf[:, unit, which * half : (which + 1) * half]
            out_ref[:, k, pl.ds(first, half), :] = rows
            out_ref[:, k, pl.ds(other, half), :] = jnp.zeros_like(rows)


def add_kernel(out_in, moved_ref, out_ref):
    out_ref[...] = out_in[...] + moved_ref[...]


def input_parts(plus, field_count, chunk):
    cuts = [k for k in range(1, plus) if k % 4 == 0 and k * field_count % 8 == 0]
    firsts = [0] + cuts
    rows = [k * field_count for k in firsts] + [min(chunk, -(-plus * field_count // 8) * 8)]
    return [(k, rows[n], rows[n + 1] - rows[n]) for n, k in enumerate(firsts)]


def cost(flops):
    return pl.CostEstimate(flops=int(flops), bytes_accessed=8 * 1024 * 1024, transcendentals=0)


def in_hbm(values):
    return pltpu.with_memory_space_constraint(values, pltpu.HBM)


def whole_spec(shape):
    zeros = (0,) * len(shape)
    return pl.BlockSpec(tuple(shape), lambda *_: zeros)


def local(tables, vorticity, forcing_mode, time_step, rotation):
    angle_local, samples, row_count, width = vorticity.shape
    phys = lax.axis_size("phys")
    ang = lax.axis_size("ang")
    angle_total = angle_local * ang
    group_fields = angle_local * samples
    field_count = -(-group_fields // phys)
    plus = tables["plus"]
    count = plus * phys
    direct = row_count == 32 and phys == 8 and group_fields % 32 == 0
    levelled = direct and width // ang == 64 and plus == 11
    units = 9 if levelled else plus
    chunk = -(-units * field_count // 8) * 8
    block = width // ang
    interleave = block == 64

    forcing = forcing_mode[0].astype(F32)
    rows_global = jnp.arange(width, dtype=jnp.int32).astype(F32)
    force = (-forcing * jnp.cos(forcing * (2 * jnp.pi * rows_global / width)))[None, :]

    fields = vorticity.reshape(group_fields, row_count, width)
    fwd = list(tables["fwd_x"]) + list(tables["fwd_y"][0]) + list(tables["fwd_y"][1])
    fwd = [jnp.asarray(t) for t in fwd]
    inv = list(tables["inv_x"]) + list(tables["inv_kx"]) + list(tables["inv_y"][0]) + list(tables["inv_y"][1])
    inv = [in_hbm(jnp.asarray(t)) for t in inv]
    def params(megabytes):
        return pltpu.CompilerParams(
            dimension_semantics=("arbitrary",), vmem_limit_bytes=megabytes * 1024 * 1024
        )

    send_shape = (4, phys * chunk, 128)
    fixed = (interleave, field_count, plus)
    send_out = pltpu.HBM(send_shape, F32)
    if direct:
        groups = field_count // 4
        fields = pl.pallas_call(
            rows_kernel,
            grid=(group_fields // 32,),
            in_specs=[pl.BlockSpec((32, row_count, width), lambda n: (n, 0, 0))]
            + [whole_spec(t.shape) for t in fwd[:2]],
            out_specs=pl.BlockSpec((8, 2 * count, 128), lambda n: (n, 0, 0)),
            out_shape=jax.ShapeDtypeStruct((group_fields // 4, 2 * count, 128), F32),
            compiler_params=params(20),
            name="rows",
        )(in_hbm(fields), *map(in_hbm, fwd[:2]))
        fields = fields.reshape(phys, groups * 2 * count, 128)
        fields = lax.all_to_all(fields, "phys", split_axis=0, concat_axis=0, tiled=True)
        spectra = fields.reshape(phys, groups, 2 * count, 128)
        spectra_spec = pl.BlockSpec((phys, 1, 2 * count, 128), lambda g: (0, g, 0, 0))
        start_send = pl.pallas_call(
            functools.partial(columns_kernel, *fixed),
            grid=(groups,),
            in_specs=[spectra_spec] + [whole_spec(t.shape) for t in fwd[2:]],
            out_specs=whole_spec(send_shape),
            out_shape=jax.ShapeDtypeStruct(send_shape, F32),
            compiler_params=params(20),
            name="columns",
        )(spectra, *fwd[2:])
        stack = 4
    else:
        extra = field_count * phys - group_fields
        fields = jnp.pad(fields, ((0, extra), (0, 0), (0, 0)))
        fields = fields.reshape(phys, field_count, row_count, width)
        fields = lax.all_to_all(fields, "phys", split_axis=0, concat_axis=0, tiled=True)
        spectra, start_send = pl.pallas_call(
            functools.partial(spectrum_kernel, *fixed),
            grid=(field_count,),
            in_specs=[pl.BlockSpec((phys, 1, row_count, width), lambda f: (0, f, 0, 0))]
            + [whole_spec(t.shape) for t in fwd],
            out_specs=[
                pl.BlockSpec((1, count, 2 * width), lambda f: (f, 0, 0)),
                whole_spec(send_shape),
            ],
            out_shape=[
                jax.ShapeDtypeStruct((field_count, count, 2 * width), F32),
                jax.ShapeDtypeStruct(send_shape, F32),
            ],
            compiler_params=params(24),
            name="spectrum",
        )(fields, *fwd)
        spectra_spec = pl.BlockSpec((1, count, 2 * width), lambda f: (f, 0, 0))
        stack = 1

    def exchange(send):
        rows = chunk
        if interleave:
            send = send.reshape(ang * phys, rows, 128)
        else:
            send = send.reshape(2, 2, phys, rows, 128 // block, block)
            send = send.transpose(1, 4, 2, 3, 0, 5).reshape(ang * phys, rows, 2 * block)
        got = lax.all_to_all(send, ("ang", "phys"), split_axis=0, concat_axis=0, tiled=True)
        return got

    start = exchange(start_send)

    extra = [force, jnp.asarray(tables["wave_x"]), jnp.asarray(tables["wave_y"])]
    adv_send = pl.pallas_call(
        functools.partial(advance_kernel, *fixed),
        grid=(field_count // stack,),
        in_specs=[
            pl.BlockSpec(memory_space=pltpu.SMEM),
            spectra_spec,
        ]
        + [whole_spec(t.shape) for t in extra + fwd + inv],
        out_specs=whole_spec(send_shape),
        out_shape=send_out,
        cost_estimate=cost(field_count * 24 * count * 6 * width * width),
        compiler_params=params(36),
        name="advance",
    )(time_step, spectra, *extra, *map(in_hbm, fwd), *inv)
    adv_send, start = lax.optimization_barrier((adv_send, start))
    advanced = exchange(adv_send)

    each = field_count // samples if field_count >= samples else field_count
    tables_s = 1 if field_count >= samples else samples
    index = np.arange(field_count)[:, None] + field_count * np.arange(phys)[None, :]
    index = np.broadcast_to(index[:, None, :], (field_count, ang, phys))
    first = np.arange(ang)[None, :, None] * angle_local + index // samples
    turn = 2.0 * math.pi / angle_total * np.mod(
        first[..., None] * np.arange(angle_total), angle_total
    )
    pair = np.concatenate([np.cos(turn), np.sin(turn)], axis=-1) / math.sqrt(angle_total)
    pair = np.where((index < group_fields)[..., None], pair, 0.0)
    matrix = []
    for s in range(tables_s):
        if tables_s == 1:
            rows = pair[::samples]
        else:
            rows = np.where((index % samples == s)[..., None], pair, 0.0)
        matrix.append(rows.reshape(each * ang * phys, 2 * angle_total).T)
    mat_hi, mat_lo = [jnp.asarray(t) for t in split_table(np.stack(matrix))]
    signed_angle = jnp.asarray(signed(np.arange(angle_total), angle_total).astype(np.float32))
    turns = jnp.stack(
        [
            jnp.tile(jnp.cos(signed_angle * rotation[0]), samples),
            jnp.tile(jnp.sin(signed_angle * rotation[0]), samples),
        ]
    )
    merged = samples * angle_total

    vmem = pl.BlockSpec(memory_space=pltpu.VMEM)
    hbm = pl.BlockSpec(memory_space=pltpu.HBM)

    def to_angles(got, last, turning, count, place=None):
        shape = (2, count, block, merged)
        parts = len(input_parts(count, field_count, chunk))
        kernel, first = functools.partial(angle_kernel, count), []
        out_spec, out_shape = hbm, pltpu.HBM(shape, F32)
        if place is not None:
            kernel, first = place_kernel, [pl.BlockSpec(memory_space=pltpu.SMEM)]
            out_spec = vmem
            out_shape = jax.ShapeDtypeStruct((2, plus, block, merged), F32)
            kernel = functools.partial(kernel, field_count, samples)
        else:
            kernel = functools.partial(kernel, field_count, samples, turning)
        return pl.pallas_call(
            kernel,
            in_specs=first + [hbm, vmem, vmem, vmem if turning else hbm],
            out_specs=out_spec,
            out_shape=out_shape,
            scratch_shapes=[
                pltpu.VMEM(got.shape, F32),
                pltpu.VMEM((8, 128) if turning else shape, F32),
                pltpu.VMEM(shape, F32),
                pltpu.VMEM((count * 2 * merged // 128, block, 128), F32),
                pltpu.SemaphoreType.DMA((parts,)),
                pltpu.SemaphoreType.DMA((parts,)),
                pltpu.SemaphoreType.DMA((count,)),
            ],
            cost_estimate=cost(2 * count * 2 * block * 3 * mat_hi.shape[2] * 2 * merged),
            compiler_params=pltpu.CompilerParams(vmem_limit_bytes=20 * 1024 * 1024),
            name="angle",
        )(*([] if place is None else [place]), got, mat_hi, mat_lo, last)

    start_part = in_hbm(to_angles(start, turns, True, units))
    if not levelled:
        return to_angles(advanced, start_part, False, units)
    extra = plus - units
    moved = lax.ppermute(
        to_angles(advanced, start_part, False, extra), "ang", [(1, 0), (2, 3)]
    )
    ang_index = lax.axis_index("ang")
    kind = jnp.where((ang_index == 0) | (ang_index == 3), 0, ang_index).astype(jnp.int32)
    out = to_angles(advanced, start_part, False, units, kind.reshape(1))
    spec = pl.BlockSpec((2, 1, block, merged), lambda k: (0, units + k, 0, 0))
    return pl.pallas_call(
        add_kernel,
        grid=(extra,),
        in_specs=[spec, pl.BlockSpec((2, 1, block, merged), lambda k: (0, k, 0, 0))],
        out_specs=spec,
        out_shape=jax.ShapeDtypeStruct(out.shape, F32),
        input_output_aliases={0: 0},
        compiler_params=params(20),
        name="add",
    )(out, moved)


def solution(mesh):
    in_specs = (P("ang", None, "phys", None), P(), P(), P())
    out_specs = P(None, "phys", "ang", None)

    def program(vorticity, forcing_mode, time_step, rotation):
        tables = make_tables(vorticity.shape[3], mesh.shape["phys"], mesh.shape["ang"])
        return jax.shard_map(
            functools.partial(local, tables),
            mesh=mesh,
            in_specs=in_specs,
            out_specs=out_specs,
            check_vma=False,
        )(vorticity, forcing_mode, time_step, rotation)

    return program
```

```python
import functools
import math

import jax
import jax.numpy as jnp
import ml_dtypes
import numpy as np
from jax import lax
from jax.experimental import pallas as pl
from jax.experimental.pallas import tpu as pltpu
from jax.sharding import PartitionSpec as P

VISCOSITY = 1.0 / 40.0
F32 = jnp.float32
BF16 = jnp.bfloat16


def split_table(table):
    table = np.asarray(table, np.float32)
    high = table.astype(ml_dtypes.bfloat16)
    low = (table - high.astype(np.float32)).astype(ml_dtypes.bfloat16)
    return high, low


def signed(values, length):
    return np.where(values < length // 2, values, values - length)


def make_tables(width, phys, ang):
    limit = width // 3
    half = width // 2
    plus = (limit + phys) // phys
    count = plus * phys
    full = 8 * phys * (plus // 8)
    row = np.arange(count)
    rest = plus % 8
    kx = np.where(
        row < full,
        (row % max(full, 1)) // 8 // max(plus // 8, 1) * plus + row % (8 * max(plus // 8, 1)),
        (row - full) // max(rest, 1) * plus + plus - rest + (row - full) % max(rest, 1),
    )
    kx_keep = (kx <= limit).astype(np.float64)
    block = width // ang
    lane = np.arange(width)
    owner = lane // block
    part = (lane % block) // (block // 2)
    even_index = owner * block + 2 * (lane % (block // 2))
    turn = 2.0 * math.pi / width
    grid = np.arange(width)

    def angle(left, right):
        return turn * np.mod(left[:, None] * right[None, :], width)

    x_turn = angle(kx, grid)
    fwd_x = np.concatenate([np.cos(x_turn), -np.sin(x_turn)]) / width
    fwd_x = fwd_x * np.concatenate([kx_keep, kx_keep])[:, None]
    weight = (np.where(kx == 0, 1.0, 2.0) * kx_keep)[:, None]
    inv_x = np.concatenate([weight * np.cos(x_turn), -weight * np.sin(x_turn)]).T
    inv_kx = np.concatenate(
        [-weight * kx[:, None] * np.sin(x_turn), -weight * kx[:, None] * np.cos(x_turn)]
    ).T
    fwd_y, inv_y, lane_ky = [], [], []
    for parity in (0, 1):
        ky = signed(even_index + parity, width)
        keep = (np.abs(ky) <= limit).astype(np.float64)
        lane_ky.append(ky)
        y_turn = angle(np.arange(half), ky)
        cos_y, sin_y = np.cos(y_turn) * keep, np.sin(y_turn) * keep
        real_out = part == 0
        from_real = np.where(real_out, cos_y, -sin_y)
        from_imag = np.where(real_out, sin_y, cos_y)
        fwd_y.append(np.concatenate([from_real, from_imag]) / width)
        real_back = np.where(real_out, cos_y, -sin_y).T
        imag_back = np.where(real_out, sin_y, cos_y).T
        scale = ky[:, None]
        inv_y.append(
            np.concatenate(
                [real_back, imag_back, -scale * imag_back, scale * real_back], axis=1
            )
        )
    return dict(
        plus=plus,
        fwd_x=split_table(fwd_x),
        inv_x=split_table(inv_x),
        inv_kx=split_table(inv_kx),
        fwd_y=[split_table(t) for t in fwd_y],
        inv_y=[split_table(t) for t in inv_y],
        wave_x=kx.astype(np.float32)[:, None],
        wave_y=np.concatenate(lane_ky).astype(np.float32)[None, :],
    )


def split(values):
    high = values.astype(BF16)
    low = (values - high.astype(F32)).astype(BF16)
    return high, low


def right_mul(values, high_ref, low_ref):
    high, low = split(values)
    left = jnp.concatenate([high, low, high], axis=1)
    right = jnp.concatenate([high_ref[...], high_ref[...], low_ref[...]], axis=0)
    return jnp.dot(left, right, preferred_element_type=F32)


def left_mul(high_ref, low_ref, values):
    high, low = split(values)
    left = jnp.concatenate([high_ref[...], low_ref[...], high_ref[...]], axis=1)
    right = jnp.concatenate([high, high, low], axis=0)
    return jnp.dot(left, right, preferred_element_type=F32)


def forward_y(rows, tables):
    count = rows.shape[0] // 2
    half = rows.shape[1] // 2
    real, imag = rows[:count], rows[count:]
    even = jnp.concatenate(
        [real[:, :half] + real[:, half:], imag[:, :half] + imag[:, half:]], axis=1
    )
    odd = jnp.concatenate(
        [real[:, :half] - real[:, half:], imag[:, :half] - imag[:, half:]], axis=1
    )
    return jnp.concatenate(
        [right_mul(even, tables[0], tables[1]), right_mul(odd, tables[2], tables[3])], axis=1
    )


def store_send(send_ref, modes, field, field_count, plus, interleave):
    pieces = [modes[:, 128 * b : 128 * (b + 1)] for b in range(4)]
    if interleave:
        low_lane = lax.broadcasted_iota(jnp.int32, pieces[0].shape, 1) < 64
        out = []
        for b in range(2):
            even, odd = pieces[b], pieces[b + 2]
            out.append(jnp.where(low_lane, even, pltpu.roll(odd, 64, 1)))
            out.append(jnp.where(low_lane, pltpu.roll(even, 64, 1), odd))
        pieces = out
    phys = modes.shape[0] // plus
    chunk = send_ref.shape[1] // phys
    if chunk < plus * field_count:
        store_levelled(send_ref, pieces, field, field_count)
        return
    whole, rest = 8 * (plus // 8), plus % 8
    for owner in range(phys):
        parts = [(owner * whole, whole, 0), (phys * whole + owner * rest, rest, whole)]
        for start, size, first in parts:
            if not size:
                continue
            place = pl.ds(owner * chunk + first * field_count + field, size, stride=field_count)
            for b in range(4):
                send_ref[b, place, :] = pieces[b][start : start + size]


def store_levelled(send_ref, pieces, field, field_count):
    phys = 8
    chunk = send_ref.shape[1] // phys
    lane = lax.broadcasted_iota(jnp.int32, pieces[0].shape, 1)
    low = lane % 32 < 16

    def pair(values, other, upper):
        if upper:
            return jnp.where(low, pltpu.roll(values, 128 - 16, 1), other)
        return jnp.where(low, values, pltpu.roll(other, 16, 1))

    def put(owner, p, unit, rows):
        place = pl.ds(p * chunk + unit * field_count + field, rows.shape[0], stride=field_count)
        send_ref[owner, place, :] = rows

    count = pieces[0].shape[0]
    for end, middle in ((0, 1), (3, 2)):
        whole, part = pieces[end], pieces[middle]
        fours = pair(part, pltpu.roll(part, count - 4, 0), middle == 2)
        ones = pair(part, pltpu.roll(part, count - 1, 0), middle == 2)
        for p in range(phys):
            tail = 64 + 3 * p
            put(end, p, 0, whole[8 * p : 8 * p + 8])
            put(end, p, 8, whole[tail : tail + 1])
            put(middle, p, 0, whole[tail + 1 : tail + 3])
            put(middle, p, 2, fours[8 * p : 8 * p + 4])
            put(middle, p, 6, ones[tail : tail + 1])
            put(middle, p, 7, ones[tail + 2 : tail + 3])


def rows_kernel(x_ref, fx_hi, fx_lo, out_ref):
    width = x_ref.shape[2]
    high, low = split(x_ref[...].reshape(-1, width))
    left = jnp.concatenate([fx_hi[...], fx_lo[...], fx_hi[...]], axis=1)
    right = jnp.concatenate([high, high, low], axis=1)
    rows = lax.dot_general(left, right, (((1,), (1,)), ((), ())), preferred_element_type=F32)
    for group in range(out_ref.shape[0]):
        out_ref[group] = rows[:, 128 * group : 128 * (group + 1)]


def swap_lanes(first, second, width):
    lane = lax.broadcasted_iota(jnp.int32, first.shape, 1)
    keep = (lane // width) % 2 == 0
    return (
        jnp.where(keep, first, pltpu.roll(second, width, 1)),
        jnp.where(keep, pltpu.roll(first, 128 - width, 1), second),
    )


def gather_rows(pieces):
    left = swap_lanes(pieces[0], pieces[2], 64)
    right = swap_lanes(pieces[1], pieces[3], 64)
    return swap_lanes(left[0], right[0], 32) + swap_lanes(left[1], right[1], 32)


def four_modes(x_ref, e_hi, e_lo, o_hi, o_lo):
    halves = [gather_rows([x_ref[4 * h + q, 0] for q in range(4)]) for h in range(2)]
    fields = [jnp.concatenate([halves[0][i], halves[1][i]], axis=1) for i in range(4)]
    count = fields[0].shape[0] // 2
    rows = jnp.concatenate([f[:count] for f in fields] + [f[count:] for f in fields], axis=0)
    modes = forward_y(rows, (e_hi, e_lo, o_hi, o_lo))
    return [modes[i * count : (i + 1) * count] for i in range(4)]


def columns_kernel(interleave, field_count, plus, x_ref, e_hi, e_lo, o_hi, o_lo, send_ref):
    modes = four_modes(x_ref, e_hi, e_lo, o_hi, o_lo)
    for i in range(4):
        field = pl.program_id(0) * 4 + i
        store_send(send_ref, modes[i], field, field_count, plus, interleave)


def spectrum_kernel(interleave, field_count, plus, x_ref, fx_hi, fx_lo, e_hi, e_lo, o_hi, o_lo, s_ref, send_ref):
    width = x_ref.shape[3]
    grid_field = x_ref[:, 0].reshape(width, width)
    high, low = split(grid_field)
    left = jnp.concatenate([fx_hi[...], fx_lo[...], fx_hi[...]], axis=1)
    right = jnp.concatenate([high, high, low], axis=1)
    rows = lax.dot_general(left, right, (((1,), (1,)), ((), ())), preferred_element_type=F32)
    modes = forward_y(rows, (e_hi, e_lo, o_hi, o_lo))
    s_ref[0] = modes
    store_send(send_ref, modes, pl.program_id(0), field_count, plus, interleave)


def advance_kernel(
    interleave,
    field_count,
    plus,
    dt_ref,
    s_ref,
    force_ref,
    wave_x_ref,
    wave_y_ref,
    fx_hi,
    fx_lo,
    e_hi,
    e_lo,
    o_hi,
    o_lo,
    bx_hi,
    bx_lo,
    bk_hi,
    bk_lo,
    ye_hi,
    ye_lo,
    yo_hi,
    yo_lo,
    send_ref,
):
    if len(s_ref.shape) == 4:
        spectra = four_modes(s_ref, e_hi, e_lo, o_hi, o_lo)
    else:
        spectra = [s_ref[i] for i in range(s_ref.shape[0])]
    stack = len(spectra)
    count, width = spectra[0].shape[0], spectra[0].shape[1] // 2
    half = width // 2
    wave_x, wave_y = wave_x_ref[...], wave_y_ref[...]
    wave_sq = wave_x * wave_x + wave_y * wave_y
    inverse_sq = jnp.where(wave_sq > 0, 1.0 / jnp.where(wave_sq > 0, wave_sq, 1.0), 0.0)
    damping = VISCOSITY * wave_sq

    def tendency(modes):
        both = jnp.concatenate([m * inverse_sq for m in modes] + modes, axis=0)
        even = right_mul(both[:, :width], ye_hi, ye_lo)
        odd = right_mul(both[:, width:], yo_hi, yo_lo)
        first, second = even + odd, even - odd

        def columns(row, block):
            rows = slice(row * count, (row + 1) * count)
            real = slice(2 * block * half, (2 * block + 1) * half)
            imag = slice((2 * block + 1) * half, (2 * block + 2) * half)
            return jnp.concatenate(
                [
                    jnp.concatenate([first[rows, real], second[rows, real]], axis=1),
                    jnp.concatenate([first[rows, imag], second[rows, imag]], axis=1),
                ],
                axis=0,
            )

        rows = []
        for i in range(stack):
            vel_x = left_mul(bx_hi, bx_lo, columns(i, 1))
            grad_x = left_mul(bk_hi, bk_lo, columns(stack + i, 0))
            total = vel_x * grad_x
            minus_vel_y = left_mul(bk_hi, bk_lo, columns(i, 0))
            grad_y = left_mul(bx_hi, bx_lo, columns(stack + i, 1))
            total = force_ref[...] - (total - minus_vel_y * grad_y)
            rows.append(left_mul(fx_hi, fx_lo, total))
        rows = jnp.concatenate([r[:count] for r in rows] + [r[count:] for r in rows], axis=0)
        out = forward_y(rows, (e_hi, e_lo, o_hi, o_lo))
        return [out[i * count : (i + 1) * count] - damping * modes[i] for i in range(stack)]

    step = dt_ref[0]
    middle = [s + (0.5 * step) * t for s, t in zip(spectra, tendency(spectra))]
    second = tendency(middle)
    for i in range(stack):
        field = pl.program_id(0) * stack + i
        advanced = spectra[i] + step * second[i]
        store_send(send_ref, advanced, field, field_count, plus, interleave)


def angle_kernel(
    plus,
    field_count,
    samples,
    turning,
    got_hbm,
    mat_hi,
    mat_lo,
    last_ref,
    out_hbm,
    got_ref,
    last_buf,
    out_buf,
    rows_ref,
    got_sem,
    last_sem,
    out_sem,
):
    sources, chunk, lanes = got_hbm.shape
    modes = mat_hi.shape[1] // 2
    quarter = lanes // 4
    merged = samples * modes
    blocks = merged // 128
    parts = input_parts(plus, field_count, chunk)
    loads = []
    for n, (first_k, first, size) in enumerate(parts):
        place = (slice(None), slice(first, first + size))
        copies = []
        if turning:
            copies = [pltpu.make_async_copy(got_hbm.at[place], got_ref.at[place], got_sem.at[n])]
        if not turning:
            last_k = parts[n + 1][0] if n + 1 < len(parts) else plus
            place = (slice(None), slice(first_k, last_k))
            copies.append(
                pltpu.make_async_copy(last_ref.at[place], last_buf.at[place], last_sem.at[n])
            )
        for copy in copies:
            copy.start()
        loads.append((first_k, copies))
    flat = (got_ref if turning else got_hbm).reshape(sources * chunk, lanes)
    stores = []
    for k in range(plus):
        for first_k, copies in loads:
            if first_k == k:
                for copy in copies:
                    copy.wait()
        cos_rows, sin_rows = [], []
        for s in range(samples):
            if field_count < samples:
                picks, table = range(field_count), s
            else:
                picks, table = range(s, field_count, samples), 0
            values = jnp.concatenate(
                [flat[pl.ds(k * field_count + f, sources, stride=chunk), :] for f in picks],
                axis=0,
            )
            result = left_mul(mat_hi.at[table], mat_lo.at[table], values)
            cos_rows.append(result[:modes])
            sin_rows.append(result[modes:])
        cosine = jnp.concatenate(cos_rows, axis=0).T
        sine = jnp.concatenate(sin_rows, axis=0).T
        for parity in range(2):
            row = parity * 2 * quarter
            near, far = slice(row, row + quarter), slice(row + quarter, row + 2 * quarter)
            real = cosine[near] + sine[far]
            imag = cosine[far] - sine[near]
            if turning:
                turn_cos, turn_sin = last_ref[0:1], last_ref[1:2]
                pair = (turn_sin * imag - turn_cos * real, -(turn_sin * real + turn_cos * imag))
            else:
                pair = (real, imag)
            for part in range(2):
                for b in range(blocks):
                    place = (k * 2 + part) * blocks + b
                    rows_ref[place, pl.ds(parity, quarter, stride=2), :] = pair[part][
                        :, 128 * b : 128 * (b + 1)
                    ]
        for part in range(2):
            place = (k * 2 + part) * blocks
            joined = jnp.concatenate([rows_ref[place + b] for b in range(blocks)], axis=1)
            out_buf[part, k] = joined if turning else joined + last_buf[part, k]
        copy = pltpu.make_async_copy(out_buf.at[:, k], out_hbm.at[:, k], out_sem.at[k])
        copy.start()
        stores.append(copy)
    for copy in stores:
        copy.wait()


def place_kernel(kind_ref, units_ref, moved_ref, out_ref):
    kind = kind_ref[0]
    units = units_ref.shape[1]
    half = out_ref.shape[2] // 2

    @pl.when(kind == 0)
    def _():
        out_ref[:, :units] = units_ref[...]
        out_ref[:, units:] = moved_ref[...]

    @pl.when(kind > 0)
    def _():
        first = pl.multiple_of((kind - 1) * half, half)
        other = pl.multiple_of(half - first, half)
        pairs = [(2 + k, 0, k) for k in range(4)] + [(2 + k, 1, 4 + k) for k in range(4)]
        pairs += [(6, 0, 8), (6, 1, 9), (7, 0, 10)]
        for unit, which, k in pairs:
            rows = units_ref[:, unit, which * half : (which + 1) * half]
            out_ref[:, k, pl.ds(first, half), :] = rows
            out_ref[:, k, pl.ds(other, half), :] = jnp.zeros_like(rows)


def input_parts(plus, field_count, chunk):
    cuts = [k for k in range(1, plus) if k % 4 == 0 and k * field_count % 8 == 0]
    firsts = [0] + cuts
    rows = [k * field_count for k in firsts] + [min(chunk, -(-plus * field_count // 8) * 8)]
    return [(k, rows[n], rows[n + 1] - rows[n]) for n, k in enumerate(firsts)]


def cost(flops):
    return pl.CostEstimate(flops=int(flops), bytes_accessed=8 * 1024 * 1024, transcendentals=0)


def in_hbm(values):
    return pltpu.with_memory_space_constraint(values, pltpu.HBM)


def whole_spec(shape):
    zeros = (0,) * len(shape)
    return pl.BlockSpec(tuple(shape), lambda *_: zeros)


def local(tables, vorticity, forcing_mode, time_step, rotation):
    angle_local, samples, row_count, width = vorticity.shape
    phys = lax.axis_size("phys")
    ang = lax.axis_size("ang")
    angle_total = angle_local * ang
    group_fields = angle_local * samples
    field_count = -(-group_fields // phys)
    plus = tables["plus"]
    count = plus * phys
    direct = row_count == 32 and phys == 8 and group_fields % 32 == 0
    levelled = direct and width // ang == 64 and plus == 11
    units = 9 if levelled else plus
    start_chunk = -(-units * field_count // 8) * 8
    chunk = -(-plus * field_count // 8) * 8
    block = width // ang
    interleave = block == 64

    forcing = forcing_mode[0].astype(F32)
    rows_global = jnp.arange(width, dtype=jnp.int32).astype(F32)
    force = (-forcing * jnp.cos(forcing * (2 * jnp.pi * rows_global / width)))[None, :]

    fields = vorticity.reshape(group_fields, row_count, width)
    fwd = list(tables["fwd_x"]) + list(tables["fwd_y"][0]) + list(tables["fwd_y"][1])
    fwd = [jnp.asarray(t) for t in fwd]
    inv = list(tables["inv_x"]) + list(tables["inv_kx"]) + list(tables["inv_y"][0]) + list(tables["inv_y"][1])
    inv = [in_hbm(jnp.asarray(t)) for t in inv]
    def params(megabytes):
        return pltpu.CompilerParams(
            dimension_semantics=("arbitrary",), vmem_limit_bytes=megabytes * 1024 * 1024
        )

    send_shape = (4, phys * chunk, 128)
    start_shape = (4, phys * start_chunk, 128)
    fixed = (interleave, field_count, plus)
    send_out = pltpu.HBM(send_shape, F32)
    if direct:
        groups = field_count // 4
        step_fields = 48 if group_fields % 48 == 0 else 32
        fields = pl.pallas_call(
            rows_kernel,
            grid=(group_fields // step_fields,),
            in_specs=[pl.BlockSpec((step_fields, row_count, width), lambda n: (n, 0, 0))]
            + [whole_spec(t.shape) for t in fwd[:2]],
            out_specs=pl.BlockSpec((step_fields // 4, 2 * count, 128), lambda n: (n, 0, 0)),
            out_shape=jax.ShapeDtypeStruct((group_fields // 4, 2 * count, 128), F32),
            compiler_params=params(20),
            name="rows",
        )(in_hbm(fields), *map(in_hbm, fwd[:2]))
        fields = fields.reshape(phys, groups * 2 * count, 128)
        fields = lax.all_to_all(fields, "phys", split_axis=0, concat_axis=0, tiled=True)
        spectra = fields.reshape(phys, groups, 2 * count, 128)
        spectra_spec = pl.BlockSpec((phys, 1, 2 * count, 128), lambda g: (0, g, 0, 0))
        start_send = pl.pallas_call(
            functools.partial(columns_kernel, *fixed),
            grid=(groups,),
            in_specs=[spectra_spec] + [whole_spec(t.shape) for t in fwd[2:]],
            out_specs=whole_spec(start_shape),
            out_shape=jax.ShapeDtypeStruct(start_shape, F32),
            compiler_params=params(20),
            name="columns",
        )(spectra, *fwd[2:])
        stack = 4
    else:
        extra = field_count * phys - group_fields
        fields = jnp.pad(fields, ((0, extra), (0, 0), (0, 0)))
        fields = fields.reshape(phys, field_count, row_count, width)
        fields = lax.all_to_all(fields, "phys", split_axis=0, concat_axis=0, tiled=True)
        spectra, start_send = pl.pallas_call(
            functools.partial(spectrum_kernel, *fixed),
            grid=(field_count,),
            in_specs=[pl.BlockSpec((phys, 1, row_count, width), lambda f: (0, f, 0, 0))]
            + [whole_spec(t.shape) for t in fwd],
            out_specs=[
                pl.BlockSpec((1, count, 2 * width), lambda f: (f, 0, 0)),
                whole_spec(send_shape),
            ],
            out_shape=[
                jax.ShapeDtypeStruct((field_count, count, 2 * width), F32),
                jax.ShapeDtypeStruct(send_shape, F32),
            ],
            compiler_params=params(24),
            name="spectrum",
        )(fields, *fwd)
        spectra_spec = pl.BlockSpec((1, count, 2 * width), lambda f: (f, 0, 0))
        stack = 1

    def exchange(send):
        rows = send.shape[1] // phys
        if interleave:
            send = send.reshape(ang * phys, rows, 128)
        else:
            send = send.reshape(2, 2, phys, rows, 128 // block, block)
            send = send.transpose(1, 4, 2, 3, 0, 5).reshape(ang * phys, rows, 2 * block)
        got = lax.all_to_all(send, ("ang", "phys"), split_axis=0, concat_axis=0, tiled=True)
        return got

    start = exchange(start_send)

    extra = [force, jnp.asarray(tables["wave_x"]), jnp.asarray(tables["wave_y"])]
    adv_send = pl.pallas_call(
        functools.partial(advance_kernel, *fixed),
        grid=(field_count // stack,),
        in_specs=[
            pl.BlockSpec(memory_space=pltpu.SMEM),
            spectra_spec,
        ]
        + [whole_spec(t.shape) for t in extra + fwd + inv],
        out_specs=whole_spec(send_shape),
        out_shape=send_out,
        cost_estimate=cost(field_count * 24 * count * 6 * width * width),
        compiler_params=params(36),
        name="advance",
    )(time_step, spectra, *extra, *map(in_hbm, fwd), *inv)
    adv_send, start = lax.optimization_barrier((adv_send, start))
    advanced = exchange(adv_send)

    each = field_count // samples if field_count >= samples else field_count
    tables_s = 1 if field_count >= samples else samples
    index = np.arange(field_count)[:, None] + field_count * np.arange(phys)[None, :]
    index = np.broadcast_to(index[:, None, :], (field_count, ang, phys))
    first = np.arange(ang)[None, :, None] * angle_local + index // samples
    turn = 2.0 * math.pi / angle_total * np.mod(
        first[..., None] * np.arange(angle_total), angle_total
    )
    pair = np.concatenate([np.cos(turn), np.sin(turn)], axis=-1) / math.sqrt(angle_total)
    pair = np.where((index < group_fields)[..., None], pair, 0.0)
    matrix = []
    for s in range(tables_s):
        if tables_s == 1:
            rows = pair[::samples]
        else:
            rows = np.where((index % samples == s)[..., None], pair, 0.0)
        matrix.append(rows.reshape(each * ang * phys, 2 * angle_total).T)
    mat_hi, mat_lo = [jnp.asarray(t) for t in split_table(np.stack(matrix))]
    signed_angle = jnp.asarray(signed(np.arange(angle_total), angle_total).astype(np.float32))
    turns = jnp.stack(
        [
            jnp.tile(jnp.cos(signed_angle * rotation[0]), samples),
            jnp.tile(jnp.sin(signed_angle * rotation[0]), samples),
        ]
    )
    merged = samples * angle_total

    vmem = pl.BlockSpec(memory_space=pltpu.VMEM)
    hbm = pl.BlockSpec(memory_space=pltpu.HBM)

    def to_angles(got, last, turning, count):
        shape = (2, count, block, merged)
        parts = len(input_parts(count, field_count, got.shape[1]))
        return pl.pallas_call(
            functools.partial(angle_kernel, count, field_count, samples, turning),
            in_specs=[hbm if turning else vmem, vmem, vmem, vmem if turning else hbm],
            out_specs=hbm,
            out_shape=pltpu.HBM(shape, F32),
            scratch_shapes=[
                pltpu.VMEM(got.shape if turning else (8, 128), F32),
                pltpu.VMEM((8, 128) if turning else shape, F32),
                pltpu.VMEM(shape, F32),
                pltpu.VMEM((count * 2 * merged // 128, block, 128), F32),
                pltpu.SemaphoreType.DMA((parts,)),
                pltpu.SemaphoreType.DMA((parts,)),
                pltpu.SemaphoreType.DMA((count,)),
            ],
            cost_estimate=cost(2 * count * 2 * block * 3 * mat_hi.shape[2] * 2 * merged),
            compiler_params=pltpu.CompilerParams(vmem_limit_bytes=20 * 1024 * 1024),
            name="angle",
        )(got, mat_hi, mat_lo, last)

    start_part = to_angles(start, turns, True, units)
    if levelled:
        moved = lax.ppermute(start_part[:, : plus - units], "ang", [(1, 0), (2, 3)])
        ang_index = lax.axis_index("ang")
        kind = jnp.where((ang_index == 0) | (ang_index == 3), 0, ang_index).astype(jnp.int32)
        start_part = pl.pallas_call(
            place_kernel,
            in_specs=[pl.BlockSpec(memory_space=pltpu.SMEM), vmem, vmem],
            out_specs=vmem,
            out_shape=jax.ShapeDtypeStruct((2, plus, block, merged), F32),
            compiler_params=pltpu.CompilerParams(vmem_limit_bytes=20 * 1024 * 1024),
            name="place",
        )(kind.reshape(1), start_part, moved)
    return to_angles(advanced, in_hbm(start_part), False, plus)


def solution(mesh):
    in_specs = (P("ang", None, "phys", None), P(), P(), P())
    out_specs = P(None, "phys", "ang", None)

    def program(vorticity, forcing_mode, time_step, rotation):
        tables = make_tables(vorticity.shape[3], mesh.shape["phys"], mesh.shape["ang"])
        return jax.shard_map(
            functools.partial(local, tables),
            mesh=mesh,
            in_specs=in_specs,
            out_specs=out_specs,
            check_vma=False,
        )(vorticity, forcing_mode, time_step, rotation)

    return program
```

```python
import functools
import math

import jax
import jax.numpy as jnp
import ml_dtypes
import numpy as np
from jax import lax
from jax.experimental import pallas as pl
from jax.experimental.pallas import tpu as pltpu
from jax.sharding import PartitionSpec as P

VISCOSITY = 1.0 / 40.0
F32 = jnp.float32
BF16 = jnp.bfloat16


def split_table(table):
    table = np.asarray(table, np.float32)
    high = table.astype(ml_dtypes.bfloat16)
    low = (table - high.astype(np.float32)).astype(ml_dtypes.bfloat16)
    return high, low


def signed(values, length):
    return np.where(values < length // 2, values, values - length)


def make_tables(width, phys, ang):
    limit = width // 3
    half = width // 2
    plus = (limit + phys) // phys
    count = plus * phys
    full = 8 * phys * (plus // 8)
    row = np.arange(count)
    rest = plus % 8
    kx = np.where(
        row < full,
        (row % max(full, 1)) // 8 // max(plus // 8, 1) * plus + row % (8 * max(plus // 8, 1)),
        (row - full) // max(rest, 1) * plus + plus - rest + (row - full) % max(rest, 1),
    )
    kx_keep = (kx <= limit).astype(np.float64)
    block = width // ang
    lane = np.arange(width)
    owner = lane // block
    part = (lane % block) // (block // 2)
    even_index = owner * block + 2 * (lane % (block // 2))
    turn = 2.0 * math.pi / width
    grid = np.arange(width)

    def angle(left, right):
        return turn * np.mod(left[:, None] * right[None, :], width)

    x_turn = angle(kx, grid)
    fwd_x = np.concatenate([np.cos(x_turn), -np.sin(x_turn)]) / width
    fwd_x = fwd_x * np.concatenate([kx_keep, kx_keep])[:, None]
    weight = (np.where(kx == 0, 1.0, 2.0) * kx_keep)[:, None]
    inv_x = np.concatenate([weight * np.cos(x_turn), -weight * np.sin(x_turn)]).T
    inv_kx = np.concatenate(
        [-weight * kx[:, None] * np.sin(x_turn), -weight * kx[:, None] * np.cos(x_turn)]
    ).T
    fwd_y, inv_y, lane_ky = [], [], []
    for parity in (0, 1):
        ky = signed(even_index + parity, width)
        keep = (np.abs(ky) <= limit).astype(np.float64)
        lane_ky.append(ky)
        y_turn = angle(np.arange(half), ky)
        cos_y, sin_y = np.cos(y_turn) * keep, np.sin(y_turn) * keep
        real_out = part == 0
        from_real = np.where(real_out, cos_y, -sin_y)
        from_imag = np.where(real_out, sin_y, cos_y)
        fwd_y.append(np.concatenate([from_real, from_imag]) / width)
        real_back = np.where(real_out, cos_y, -sin_y).T
        imag_back = np.where(real_out, sin_y, cos_y).T
        scale = ky[:, None]
        inv_y.append(
            np.concatenate(
                [real_back, imag_back, -scale * imag_back, scale * real_back], axis=1
            )
        )
    return dict(
        plus=plus,
        fwd_x=split_table(fwd_x),
        inv_x=split_table(inv_x),
        inv_kx=split_table(inv_kx),
        fwd_y=[split_table(t) for t in fwd_y],
        inv_y=[split_table(t) for t in inv_y],
        wave_x=kx.astype(np.float32)[:, None],
        wave_y=np.concatenate(lane_ky).astype(np.float32)[None, :],
    )


def split(values):
    high = values.astype(BF16)
    low = (values - high.astype(F32)).astype(BF16)
    return high, low


def right_mul(values, high_ref, low_ref):
    high, low = split(values)
    left = jnp.concatenate([high, low, high], axis=1)
    right = jnp.concatenate([high_ref[...], high_ref[...], low_ref[...]], axis=0)
    return jnp.dot(left, right, preferred_element_type=F32)


def left_mul(high_ref, low_ref, values):
    high, low = split(values)
    left = jnp.concatenate([high_ref[...], low_ref[...], high_ref[...]], axis=1)
    right = jnp.concatenate([high, high, low], axis=0)
    return jnp.dot(left, right, preferred_element_type=F32)


def forward_y(rows, tables):
    count = rows.shape[0] // 2
    half = rows.shape[1] // 2
    real, imag = rows[:count], rows[count:]
    even = jnp.concatenate(
        [real[:, :half] + real[:, half:], imag[:, :half] + imag[:, half:]], axis=1
    )
    odd = jnp.concatenate(
        [real[:, :half] - real[:, half:], imag[:, :half] - imag[:, half:]], axis=1
    )
    return jnp.concatenate(
        [right_mul(even, tables[0], tables[1]), right_mul(odd, tables[2], tables[3])], axis=1
    )


def store_send(send_ref, modes, field, field_count, plus, interleave, start=None):
    def owners(values):
        pieces = [values[:, 128 * b : 128 * (b + 1)] for b in range(4)]
        if not interleave:
            return pieces
        low_lane = lax.broadcasted_iota(jnp.int32, pieces[0].shape, 1) < 64
        out = []
        for b in range(2):
            even, odd = pieces[b], pieces[b + 2]
            out.append(jnp.where(low_lane, even, pltpu.roll(odd, 64, 1)))
            out.append(jnp.where(low_lane, pltpu.roll(even, 64, 1), odd))
        return out

    pieces = owners(modes)
    if start is not None:
        start = owners(start)
        pieces[1] = pair_lanes(pieces[1], start[1], False)
        pieces[2] = pair_lanes(pieces[2], start[2], True)
    phys = modes.shape[0] // plus
    chunk = send_ref.shape[1] // phys
    if chunk < plus * field_count:
        store_levelled(send_ref, pieces, field, field_count)
        return
    whole, rest = 8 * (plus // 8), plus % 8
    for owner in range(phys):
        parts = [(owner * whole, whole, 0), (phys * whole + owner * rest, rest, whole)]
        for start, size, first in parts:
            if not size:
                continue
            place = pl.ds(owner * chunk + first * field_count + field, size, stride=field_count)
            for b in range(4):
                send_ref[b, place, :] = pieces[b][start : start + size]


def pair_lanes(values, other, upper):
    lane = lax.broadcasted_iota(jnp.int32, values.shape, 1)
    if upper:
        return jnp.where(lane % 32 < 16, pltpu.roll(values, 128 - 16, 1), other)
    return jnp.where(lane % 32 < 16, values, pltpu.roll(other, 16, 1))


def store_levelled(send_ref, pieces, field, field_count):
    phys = 8
    chunk = send_ref.shape[1] // phys
    own = chunk // field_count

    def put(owner, p, unit, rows):
        place = pl.ds(p * chunk + unit * field_count + field, rows.shape[0], stride=field_count)
        send_ref[owner, place, :] = rows

    for end, middle in ((0, 1), (3, 2)):
        whole = pieces[end]
        for p in range(phys):
            put(end, p, 0, whole[8 * p : 8 * p + own])
            if own < 8:
                put(middle, p, 0, whole[8 * p + own : 8 * p + 8])
            put(middle, p, 8 - own, whole[64 + 3 * p : 67 + 3 * p])


def rows_kernel(x_ref, fx_hi, fx_lo, out_ref):
    width = x_ref.shape[2]
    high, low = split(x_ref[...].reshape(-1, width))
    left = jnp.concatenate([fx_hi[...], fx_lo[...], fx_hi[...]], axis=1)
    right = jnp.concatenate([high, high, low], axis=1)
    rows = lax.dot_general(left, right, (((1,), (1,)), ((), ())), preferred_element_type=F32)
    for group in range(out_ref.shape[0]):
        out_ref[group] = rows[:, 128 * group : 128 * (group + 1)]


def swap_lanes(first, second, width):
    lane = lax.broadcasted_iota(jnp.int32, first.shape, 1)
    keep = (lane // width) % 2 == 0
    return (
        jnp.where(keep, first, pltpu.roll(second, width, 1)),
        jnp.where(keep, pltpu.roll(first, 128 - width, 1), second),
    )


def gather_rows(pieces):
    left = swap_lanes(pieces[0], pieces[2], 64)
    right = swap_lanes(pieces[1], pieces[3], 64)
    return swap_lanes(left[0], right[0], 32) + swap_lanes(left[1], right[1], 32)


def four_modes(x_ref, e_hi, e_lo, o_hi, o_lo):
    halves = [gather_rows([x_ref[4 * h + q, 0] for q in range(4)]) for h in range(2)]
    fields = [jnp.concatenate([halves[0][i], halves[1][i]], axis=1) for i in range(4)]
    count = fields[0].shape[0] // 2
    rows = jnp.concatenate([f[:count] for f in fields] + [f[count:] for f in fields], axis=0)
    modes = forward_y(rows, (e_hi, e_lo, o_hi, o_lo))
    return [modes[i * count : (i + 1) * count] for i in range(4)]


def columns_kernel(interleave, field_count, plus, x_ref, e_hi, e_lo, o_hi, o_lo, send_ref):
    modes = four_modes(x_ref, e_hi, e_lo, o_hi, o_lo)
    for i in range(4):
        field = pl.program_id(0) * 4 + i
        store_send(send_ref, modes[i], field, field_count, plus, interleave)


def spectrum_kernel(interleave, field_count, plus, x_ref, fx_hi, fx_lo, e_hi, e_lo, o_hi, o_lo, s_ref, send_ref):
    width = x_ref.shape[3]
    grid_field = x_ref[:, 0].reshape(width, width)
    high, low = split(grid_field)
    left = jnp.concatenate([fx_hi[...], fx_lo[...], fx_hi[...]], axis=1)
    right = jnp.concatenate([high, high, low], axis=1)
    rows = lax.dot_general(left, right, (((1,), (1,)), ((), ())), preferred_element_type=F32)
    modes = forward_y(rows, (e_hi, e_lo, o_hi, o_lo))
    s_ref[0] = modes
    store_send(send_ref, modes, pl.program_id(0), field_count, plus, interleave)


def advance_kernel(
    levelled,
    interleave,
    field_count,
    plus,
    dt_ref,
    s_ref,
    force_ref,
    wave_x_ref,
    wave_y_ref,
    fx_hi,
    fx_lo,
    e_hi,
    e_lo,
    o_hi,
    o_lo,
    bx_hi,
    bx_lo,
    bk_hi,
    bk_lo,
    ye_hi,
    ye_lo,
    yo_hi,
    yo_lo,
    send_ref,
):
    if len(s_ref.shape) == 4:
        spectra = four_modes(s_ref, e_hi, e_lo, o_hi, o_lo)
    else:
        spectra = [s_ref[i] for i in range(s_ref.shape[0])]
    stack = len(spectra)
    count, width = spectra[0].shape[0], spectra[0].shape[1] // 2
    half = width // 2
    wave_x, wave_y = wave_x_ref[...], wave_y_ref[...]
    wave_sq = wave_x * wave_x + wave_y * wave_y
    inverse_sq = jnp.where(wave_sq > 0, 1.0 / jnp.where(wave_sq > 0, wave_sq, 1.0), 0.0)
    damping = VISCOSITY * wave_sq

    def tendency(modes):
        both = jnp.concatenate([m * inverse_sq for m in modes] + modes, axis=0)
        even = right_mul(both[:, :width], ye_hi, ye_lo)
        odd = right_mul(both[:, width:], yo_hi, yo_lo)
        first, second = even + odd, even - odd

        def columns(row, block):
            rows = slice(row * count, (row + 1) * count)
            real = slice(2 * block * half, (2 * block + 1) * half)
            imag = slice((2 * block + 1) * half, (2 * block + 2) * half)
            return jnp.concatenate(
                [
                    jnp.concatenate([first[rows, real], second[rows, real]], axis=1),
                    jnp.concatenate([first[rows, imag], second[rows, imag]], axis=1),
                ],
                axis=0,
            )

        rows = []
        for i in range(stack):
            vel_x = left_mul(bx_hi, bx_lo, columns(i, 1))
            grad_x = left_mul(bk_hi, bk_lo, columns(stack + i, 0))
            total = vel_x * grad_x
            minus_vel_y = left_mul(bk_hi, bk_lo, columns(i, 0))
            grad_y = left_mul(bx_hi, bx_lo, columns(stack + i, 1))
            total = force_ref[...] - (total - minus_vel_y * grad_y)
            rows.append(left_mul(fx_hi, fx_lo, total))
        rows = jnp.concatenate([r[:count] for r in rows] + [r[count:] for r in rows], axis=0)
        out = forward_y(rows, (e_hi, e_lo, o_hi, o_lo))
        return [out[i * count : (i + 1) * count] - damping * modes[i] for i in range(stack)]

    step = dt_ref[0]
    middle = [s + (0.5 * step) * t for s, t in zip(spectra, tendency(spectra))]
    second = tendency(middle)
    for i in range(stack):
        field = pl.program_id(0) * stack + i
        advanced = spectra[i] + step * second[i]
        start = spectra[i] if levelled else None
        store_send(send_ref, advanced, field, field_count, plus, interleave, start)


def angle_kernel(
    plus,
    field_count,
    samples,
    turning,
    kind_ref,
    turn_ref,
    got_hbm,
    mat_hi,
    mat_lo,
    last_ref,
    out_hbm,
    got_ref,
    last_buf,
    out_buf,
    rows_ref,
    got_sem,
    last_sem,
    out_sem,
):
    sources, chunk, lanes = got_hbm.shape
    modes = mat_hi.shape[1] // 2
    quarter = lanes // 4
    merged = samples * modes
    blocks = merged // 128
    parts = input_parts(plus, field_count, chunk)
    loads = []
    for n, (first_k, first, size) in enumerate(parts):
        place = (slice(None), slice(first, first + size))
        copies = []
        if turning:
            copies = [pltpu.make_async_copy(got_hbm.at[place], got_ref.at[place], got_sem.at[n])]
        if not turning:
            last_k = parts[n + 1][0] if n + 1 < len(parts) else plus
            place = (slice(None), slice(first_k, last_k))
            copies.append(
                pltpu.make_async_copy(last_ref.at[place], last_buf.at[place], last_sem.at[n])
            )
        for copy in copies:
            copy.start()
        loads.append((first_k, copies))
    turn_cos, turn_sin = turn_ref[0:1], turn_ref[1:2]
    kind = None if kind_ref is None else kind_ref[0]

    def turned_back(real, imag):
        return [turn_sin * imag - turn_cos * real, -(turn_sin * real + turn_cos * imag)]

    flat = (got_ref if turning else got_hbm).reshape(sources * chunk, lanes)
    stores = []
    for k in range(plus):
        for first_k, copies in loads:
            if first_k == k:
                for copy in copies:
                    copy.wait()
        cos_rows, sin_rows = [], []
        for s in range(samples):
            if field_count < samples:
                picks, table = range(field_count), s
            else:
                picks, table = range(s, field_count, samples), 0
            values = jnp.concatenate(
                [flat[pl.ds(k * field_count + f, sources, stride=chunk), :] for f in picks],
                axis=0,
            )
            result = left_mul(mat_hi.at[table], mat_lo.at[table], values)
            cos_rows.append(result[:modes])
            sin_rows.append(result[modes:])
        cosine = jnp.concatenate(cos_rows, axis=0).T
        sine = jnp.concatenate(sin_rows, axis=0).T
        for parity in range(2):
            row = parity * 2 * quarter
            near, far = slice(row, row + quarter), slice(row + quarter, row + 2 * quarter)
            real = cosine[near] + sine[far]
            imag = cosine[far] - sine[near]
            pair = (real, imag)
            if turning:
                pair = turned_back(real, imag)
            elif kind_ref is not None:
                half = quarter // 2
                late = turned_back(real[half:], imag[half:])
                for part in range(2):
                    own = pair[part][:half] + late[part]
                    none = jnp.zeros_like(own)
                    own = jnp.where(
                        kind == 1,
                        jnp.concatenate([own, none], axis=0),
                        jnp.concatenate([none, own], axis=0),
                    )
                    late[part] = jnp.where(kind == 0, pair[part], own)
                pair = late
            for part in range(2):
                for b in range(blocks):
                    place = (k * 2 + part) * blocks + b
                    rows_ref[place, pl.ds(parity, quarter, stride=2), :] = pair[part][
                        :, 128 * b : 128 * (b + 1)
                    ]
        for part in range(2):
            place = (k * 2 + part) * blocks
            joined = jnp.concatenate([rows_ref[place + b] for b in range(blocks)], axis=1)
            out_buf[part, k] = joined if turning else joined + last_buf[part, k]
        copy = pltpu.make_async_copy(out_buf.at[:, k], out_hbm.at[:, k], out_sem.at[k])
        copy.start()
        stores.append(copy)
    for copy in stores:
        copy.wait()


def place_kernel(kind_ref, units_ref, moved_ref, out_ref):
    kind = kind_ref[0]
    units = units_ref.shape[1]
    rest = out_ref.shape[1] - units

    @pl.when(kind == 0)
    def _():
        out_ref[:, :units] = units_ref[...]
        out_ref[:, units:] = moved_ref[:, :rest]

    @pl.when(kind > 0)
    def _():
        out_ref[...] = jnp.zeros_like(out_ref)


def input_parts(plus, field_count, chunk):
    cuts = [k for k in range(1, plus) if k % 4 == 0 and k * field_count % 8 == 0]
    firsts = [0] + cuts
    rows = [k * field_count for k in firsts] + [min(chunk, -(-plus * field_count // 8) * 8)]
    return [(k, rows[n], rows[n + 1] - rows[n]) for n, k in enumerate(firsts)]


def cost(flops):
    return pl.CostEstimate(flops=int(flops), bytes_accessed=8 * 1024 * 1024, transcendentals=0)


def in_hbm(values):
    return pltpu.with_memory_space_constraint(values, pltpu.HBM)


def whole_spec(shape):
    zeros = (0,) * len(shape)
    return pl.BlockSpec(tuple(shape), lambda *_: zeros)


def local(tables, vorticity, forcing_mode, time_step, rotation):
    angle_local, samples, row_count, width = vorticity.shape
    phys = lax.axis_size("phys")
    ang = lax.axis_size("ang")
    angle_total = angle_local * ang
    group_fields = angle_local * samples
    field_count = -(-group_fields // phys)
    plus = tables["plus"]
    count = plus * phys
    direct = row_count == 32 and phys == 8 and group_fields % 32 == 0
    levelled = direct and width // ang == 64 and plus == 11
    units = 8 if levelled else plus
    start_chunk = -(-units * field_count // 8) * 8
    chunk = -(-plus * field_count // 8) * 8
    block = width // ang
    interleave = block == 64

    forcing = forcing_mode[0].astype(F32)
    rows_global = jnp.arange(width, dtype=jnp.int32).astype(F32)
    force = (-forcing * jnp.cos(forcing * (2 * jnp.pi * rows_global / width)))[None, :]

    fields = vorticity.reshape(group_fields, row_count, width)
    fwd = list(tables["fwd_x"]) + list(tables["fwd_y"][0]) + list(tables["fwd_y"][1])
    fwd = [jnp.asarray(t) for t in fwd]
    inv = list(tables["inv_x"]) + list(tables["inv_kx"]) + list(tables["inv_y"][0]) + list(tables["inv_y"][1])
    inv = [in_hbm(jnp.asarray(t)) for t in inv]
    def params(megabytes):
        return pltpu.CompilerParams(
            dimension_semantics=("arbitrary",), vmem_limit_bytes=megabytes * 1024 * 1024
        )

    send_shape = (4, phys * chunk, 128)
    start_shape = (4, phys * start_chunk, 128)
    fixed = (interleave, field_count, plus)
    send_out = pltpu.HBM(send_shape, F32)
    if direct:
        groups = field_count // 4
        step_fields = 48 if group_fields % 48 == 0 else 32
        fields = pl.pallas_call(
            rows_kernel,
            grid=(group_fields // step_fields,),
            in_specs=[pl.BlockSpec((step_fields, row_count, width), lambda n: (n, 0, 0))]
            + [whole_spec(t.shape) for t in fwd[:2]],
            out_specs=pl.BlockSpec((step_fields // 4, 2 * count, 128), lambda n: (n, 0, 0)),
            out_shape=jax.ShapeDtypeStruct((group_fields // 4, 2 * count, 128), F32),
            compiler_params=params(20),
            name="rows",
        )(in_hbm(fields), *map(in_hbm, fwd[:2]))
        fields = fields.reshape(phys, groups * 2 * count, 128)
        fields = lax.all_to_all(fields, "phys", split_axis=0, concat_axis=0, tiled=True)
        spectra = fields.reshape(phys, groups, 2 * count, 128)
        spectra_spec = pl.BlockSpec((phys, 1, 2 * count, 128), lambda g: (0, g, 0, 0))
        start_send = pl.pallas_call(
            functools.partial(columns_kernel, *fixed),
            grid=(groups,),
            in_specs=[spectra_spec] + [whole_spec(t.shape) for t in fwd[2:]],
            out_specs=whole_spec(start_shape),
            out_shape=jax.ShapeDtypeStruct(start_shape, F32),
            compiler_params=params(20),
            name="columns",
        )(spectra, *fwd[2:])
        stack = 4
    else:
        extra = field_count * phys - group_fields
        fields = jnp.pad(fields, ((0, extra), (0, 0), (0, 0)))
        fields = fields.reshape(phys, field_count, row_count, width)
        fields = lax.all_to_all(fields, "phys", split_axis=0, concat_axis=0, tiled=True)
        spectra, start_send = pl.pallas_call(
            functools.partial(spectrum_kernel, *fixed),
            grid=(field_count,),
            in_specs=[pl.BlockSpec((phys, 1, row_count, width), lambda f: (0, f, 0, 0))]
            + [whole_spec(t.shape) for t in fwd],
            out_specs=[
                pl.BlockSpec((1, count, 2 * width), lambda f: (f, 0, 0)),
                whole_spec(send_shape),
            ],
            out_shape=[
                jax.ShapeDtypeStruct((field_count, count, 2 * width), F32),
                jax.ShapeDtypeStruct(send_shape, F32),
            ],
            compiler_params=params(24),
            name="spectrum",
        )(fields, *fwd)
        spectra_spec = pl.BlockSpec((1, count, 2 * width), lambda f: (f, 0, 0))
        stack = 1

    def exchange(send):
        rows = send.shape[1] // phys
        if interleave:
            send = send.reshape(ang * phys, rows, 128)
        else:
            send = send.reshape(2, 2, phys, rows, 128 // block, block)
            send = send.transpose(1, 4, 2, 3, 0, 5).reshape(ang * phys, rows, 2 * block)
        got = lax.all_to_all(send, ("ang", "phys"), split_axis=0, concat_axis=0, tiled=True)
        return got

    start = exchange(start_send)

    extra = [force, jnp.asarray(tables["wave_x"]), jnp.asarray(tables["wave_y"])]
    adv_send = pl.pallas_call(
        functools.partial(advance_kernel, levelled, *fixed),
        grid=(field_count // stack,),
        in_specs=[
            pl.BlockSpec(memory_space=pltpu.SMEM),
            spectra_spec,
        ]
        + [whole_spec(t.shape) for t in extra + fwd + inv],
        out_specs=whole_spec(send_shape),
        out_shape=send_out,
        cost_estimate=cost(field_count * 24 * count * 6 * width * width),
        compiler_params=params(36),
        name="advance",
    )(time_step, spectra, *extra, *map(in_hbm, fwd), *inv)
    adv_send, start = lax.optimization_barrier((adv_send, start))
    advanced = exchange(adv_send)

    each = field_count // samples if field_count >= samples else field_count
    tables_s = 1 if field_count >= samples else samples
    index = np.arange(field_count)[:, None] + field_count * np.arange(phys)[None, :]
    index = np.broadcast_to(index[:, None, :], (field_count, ang, phys))
    first = np.arange(ang)[None, :, None] * angle_local + index // samples
    turn = 2.0 * math.pi / angle_total * np.mod(
        first[..., None] * np.arange(angle_total), angle_total
    )
    pair = np.concatenate([np.cos(turn), np.sin(turn)], axis=-1) / math.sqrt(angle_total)
    pair = np.where((index < group_fields)[..., None], pair, 0.0)
    matrix = []
    for s in range(tables_s):
        if tables_s == 1:
            rows = pair[::samples]
        else:
            rows = np.where((index % samples == s)[..., None], pair, 0.0)
        matrix.append(rows.reshape(each * ang * phys, 2 * angle_total).T)
    mat_hi, mat_lo = [jnp.asarray(t) for t in split_table(np.stack(matrix))]
    signed_angle = jnp.asarray(signed(np.arange(angle_total), angle_total).astype(np.float32))
    turns = jnp.stack(
        [
            jnp.tile(jnp.cos(signed_angle * rotation[0]), samples),
            jnp.tile(jnp.sin(signed_angle * rotation[0]), samples),
        ]
    )
    merged = samples * angle_total

    vmem = pl.BlockSpec(memory_space=pltpu.VMEM)
    hbm = pl.BlockSpec(memory_space=pltpu.HBM)

    ang_index = lax.axis_index("ang")
    kind = jnp.where((ang_index == 0) | (ang_index == 3), 0, ang_index).astype(jnp.int32)
    kind = kind.reshape(1)
    smem = pl.BlockSpec(memory_space=pltpu.SMEM)

    def to_angles(got, last, count):
        turning = last is None
        shape = (2, count, block, merged)
        parts = len(input_parts(count, field_count, got.shape[1]))
        kernel = functools.partial(angle_kernel, count, field_count, samples, turning)
        operands = [(turns, vmem), (got, hbm if turning else vmem), (mat_hi, vmem), (mat_lo, vmem)]
        if turning:
            body = lambda turn, got, hi, lo, *rest: kernel(None, turn, got, hi, lo, None, *rest)
        else:
            operands.append((last, hbm))
            if levelled:
                operands.insert(0, (kind, smem))
                body = kernel
            else:
                body = functools.partial(kernel, None)
        return pl.pallas_call(
            body,
            in_specs=[spec for _, spec in operands],
            out_specs=hbm,
            out_shape=pltpu.HBM(shape, F32),
            scratch_shapes=[
                pltpu.VMEM(got.shape if turning else (8, 128), F32),
                pltpu.VMEM((8, 128) if turning else shape, F32),
                pltpu.VMEM(shape, F32),
                pltpu.VMEM((count * 2 * merged // 128, block, 128), F32),
                pltpu.SemaphoreType.DMA((parts,)),
                pltpu.SemaphoreType.DMA((parts,)),
                pltpu.SemaphoreType.DMA((count,)),
            ],
            cost_estimate=cost(2 * count * 2 * block * 3 * mat_hi.shape[2] * 2 * merged),
            compiler_params=pltpu.CompilerParams(vmem_limit_bytes=20 * 1024 * 1024),
            name="angle",
        )(*[value for value, _ in operands])

    start_part = to_angles(start, None, units)
    if levelled:
        moved = lax.ppermute(start_part[:, : plus - units], "ang", [(1, 0), (2, 3)])
        start_part = pl.pallas_call(
            place_kernel,
            in_specs=[smem, vmem, vmem],
            out_specs=vmem,
            out_shape=jax.ShapeDtypeStruct((2, plus, block, merged), F32),
            compiler_params=pltpu.CompilerParams(vmem_limit_bytes=20 * 1024 * 1024),
            name="place",
        )(kind, start_part, moved)
    return to_angles(advanced, in_hbm(start_part), plus)


def solution(mesh):
    in_specs = (P("ang", None, "phys", None), P(), P(), P())
    out_specs = P(None, "phys", "ang", None)

    def program(vorticity, forcing_mode, time_step, rotation):
        tables = make_tables(vorticity.shape[3], mesh.shape["phys"], mesh.shape["ang"])
        return jax.shard_map(
            functools.partial(local, tables),
            mesh=mesh,
            in_specs=in_specs,
            out_specs=out_specs,
            check_vma=False,
        )(vorticity, forcing_mode, time_step, rotation)

    return program
```
